32 devices in a mesh: win: 2 (over x), tmpl: 8 (over z, y), tm: 2 (over core).
Axes of the slice: x: 2, y: 2, z: 4, core: 2. Of those that a mesh axis runs over, the one named last changes fastest.
Arguments:
- records: bfloat16 [96, 4096], P('tmpl', ('win', 'tm')), parts along dimension 1, may hold values from -500 to 500
- record_tail: bfloat16 [96, 260], P(None, 'win'), parts along dimension 1, may hold values from -18 to 18
- templates: bfloat16 [2048, 9600], P('tmpl', 'tm'), may hold values from -6 to 6
- channel_mask: int32 [2048, 96], P('tmpl'), may hold values from 0 to 1, as said below
- lag_shift: int32 [192], P('win'), parts along dimension 0, may hold values from 0 to 31
Outputs:
- detection: float32 [2048, 4096], P('tmpl', ('win', 'tm')), parts along dimension 1
The draws below stay inside these ranges and needn't reach their ends.
There are 2 independent parts, one for each index of `win`. The reference program is written for one: setup_inputs(seed, part) draws one part's arguments, and reference() takes and returns one part's arrays. A program takes and returns all parts, laid end to end along the dimension named above; an argument that names none is the same for every part. Nothing has to cross between parts.
Inputs may be any that keep to these rules, and one draw needn't show every extreme that they name: `channel_mask`: every template uses at least one channel.
All inputs are finite; a program needn't handle non-finite values.
Results may differ from the reference program's by a relative error of at most 0.0042.
Values may be sent and summed in bfloat16 or wider, within the bound.
No kernel may reach another device: no remote copies, remote signals or barrier semaphores. Data moves between devices by JAX's collectives and lax.ppermute only.
A program may use at most 128 MiB of HBM per device.

```python
import math
import jax
import jax.numpy as jnp
from jax import lax

C = 96
K = 2048
L = 100
LAGS = 32
NT = 2048
TAIL = 130


def draw_records(key, part):
    keys = jax.random.split(key, 3)
    channel_scale = jnp.exp(jax.random.uniform(keys[1], (C, 1), jnp.float32, 0.0, math.log(10.0)))
    segment_scale = jnp.exp(jax.random.uniform(keys[2], (C, NT // 25 + 1), jnp.float32, 0.0, math.log(10.0)))
    position = jnp.arange(NT, dtype=jnp.int32)
    envelope = segment_scale[:, position // 25]
    base = jax.random.truncated_normal(keys[0], -4.0, 4.0, (C, NT), jnp.float32)
    return (base * envelope * channel_scale).astype(jnp.bfloat16)


def draw_channel_mask(key, part):
    keys = jax.random.split(key, 3)
    chance = jax.random.randint(keys[0], (K, 1), 3, 10)
    rolls = jax.random.randint(keys[1], (K, C), 0, 10)
    forced = jax.random.randint(keys[2], (K, 1), 0, C)
    column = jnp.arange(C, dtype=jnp.int32)[None, :]
    chosen = (rolls < chance) | (column == forced)
    return chosen.astype(jnp.int32)


def draw_lag_shift(key, part):
    keys = jax.random.split(key, 2)
    shifts = jax.random.randint(keys[0], (C,), 0, LAGS)
    forced = jax.random.randint(keys[1], (), 0, C)
    column = jnp.arange(C, dtype=jnp.int32)
    shifts = jnp.where(column == forced, LAGS - 1, shifts)
    shifts = jnp.where(column == (forced + 1) % C, 0, shifts)
    return shifts.astype(jnp.int32)


def shard_levels(key, dims, pieces, least, high):
    factor_of = 1.0
    for axis_at, parts in pieces:
        steps = jax.random.uniform(jax.random.fold_in(jax.random.fold_in(key, 6), axis_at), (parts,), jnp.float32, least / len(pieces), high / len(pieces))
        factor_of = factor_of * jnp.repeat(jnp.exp(steps), dims[axis_at] // parts).reshape((-1,) + (1,) * (len(dims) - 1 - axis_at))
    return factor_of


def gaussian(rng, shape, deviation, reach, shards=(), kind=jnp.bfloat16):
    drawn = deviation * jax.random.normal(rng, shape, jnp.float32)
    if shards:
        drawn = drawn * shard_levels(rng, shape, shards, -0.22, 0.18)
    return jnp.clip(drawn, -reach, reach).astype(kind)


def setup_inputs(seed: int = 0, part: int = 0) -> dict:
    streams_of = jax.random.split(jax.random.key(seed), 6)
    part_keys = jax.random.split(jax.random.fold_in(streams_of[5], part), 6)
    records = draw_records(jax.random.fold_in(jax.random.fold_in(streams_of[5], part), 71), part)
    record_tail = gaussian(part_keys[1], (C, TAIL), 3.0, 18.0)
    templates = gaussian(streams_of[2], (K, C * L), 1.0, 6.0, ((0, 8), (1, 2)))
    channel_mask = draw_channel_mask(jax.random.fold_in(streams_of[5], 71), part)
    lag_shift = draw_lag_shift(jax.random.fold_in(jax.random.fold_in(streams_of[5], part), 71), part)
    return {"records": records, "record_tail": record_tail, "templates": templates, "channel_mask": channel_mask, "lag_shift": lag_shift}


EPSILON = 1e-05

def energy_scale(extended, positions):
    values = extended.astype(jnp.float32)
    first = jnp.zeros((values.shape[0], positions), jnp.float32)
    second = jnp.zeros((values.shape[0], positions), jnp.float32)
    for offset in range(L):
        piece = values[:, offset:offset + positions]
        first = first + piece
        second = second + piece * piece
    return lax.rsqrt(second - first * first / L + L * EPSILON)

def reference(records, record_tail, templates, channel_mask, lag_shift):
    extended = jnp.concatenate([records, record_tail], axis=1)
    inv_energy = energy_scale(extended, NT + LAGS - 1)
    shifts = lag_shift.astype(jnp.int32)
    aligned = jax.vmap(lambda values, shift_by: lax.dynamic_slice_in_dim(values, shift_by, NT + L - 1))(extended, shifts)
    aligned_inv = jax.vmap(lambda values, shift_by: lax.dynamic_slice_in_dim(values, shift_by, NT))(inv_energy, shifts)
    shaped = templates.astype(jnp.float32).reshape(K, C, L)
    centred = shaped - lax.optimization_barrier(jnp.mean(shaped, axis=2, keepdims=True))
    unit = centred * lax.rsqrt(lax.optimization_barrier(jnp.sum(centred * centred, axis=2, keepdims=True)) + EPSILON)
    used = channel_mask.astype(jnp.float32)
    panel = (unit * used[:, :, None]).astype(jnp.bfloat16).reshape(K, C * L)
    weight_scale = jnp.sqrt(L / lax.optimization_barrier(jnp.sum(used, axis=1)))
    block_len = 512 if NT % 512 == 0 else NT

    def one_block(start):
        window = lax.dynamic_slice_in_dim(aligned, start, block_len + L - 1, 1).astype(jnp.float32)
        norms = lax.dynamic_slice_in_dim(aligned_inv, start, block_len, 1)
        hankel = jnp.stack([window[:, offset:offset + block_len] for offset in range(L)], axis=1) * norms[:, None, :]
        hankel = hankel.astype(jnp.bfloat16).reshape(C * L, block_len)
        return jnp.dot(panel, hankel, preferred_element_type=jnp.float32) * weight_scale[:, None]
    starts = jnp.arange(NT // block_len, dtype=jnp.int32) * block_len
    blocks = lax.map(one_block, starts)
    return jnp.moveaxis(blocks, 0, 1).reshape(K, NT)
```

```python
import functools

import jax
import jax.numpy as jnp
from jax import lax
from jax.experimental import pallas as pl
from jax.experimental.pallas import tpu as pltpu
from jax.sharding import PartitionSpec as P

L = 100
LAGS = 32
EPSILON = 1e-05

LANES = 128
RUN = 16
STEP = 12
ROWS = STEP * L
DEPTH = 1280
BLOCKS = 8
SPANS = 9
TILES = 14


def lane_of(shape):
    return lax.broadcasted_iota(jnp.int32, shape, len(shape) - 1)


def row_of(shape):
    return lax.broadcasted_iota(jnp.int32, shape, 0)


def natural(index):
    return (index & ~(RUN - 1)) + (RUN - 1) - (index & (RUN - 1))


def mirrored(x):
    return jnp.take_along_axis(x, natural(lane_of(x.shape)), axis=1)


def swap_runs(blocks):
    blocks = list(blocks)
    lane = lane_of(blocks[0].shape)
    for bit in range(3):
        step = RUN << bit
        upper = (lane & step) != 0
        for at in range(BLOCKS):
            if at & (1 << bit):
                continue
            low, high = blocks[at], blocks[at | (1 << bit)]
            blocks[at] = jnp.where(upper, pltpu.roll(high, step, 1), low)
            blocks[at | (1 << bit)] = jnp.where(upper, high, pltpu.roll(low, LANES - step, 1))
    return blocks


def sheared(x, first):
    return pltpu.roll(x, first % LANES, 1, stride=1, stride_axis=0)


def align_kernel(channels, place, lags, records, following, tail, out, tails, rows):
    tails[...] = jnp.zeros_like(tails)
    count = tail.shape[0]
    width = tail.shape[1]
    whole = tail[...].astype(jnp.float32)
    tails[0, pl.ds(0, count), :] = whole[:, :LANES]
    tails[1, pl.ds(0, count), pl.ds(0, width - LANES)] = whole[:, LANES:]
    own = records[...].astype(jnp.float32)
    after = following[:, : 2 * LANES].astype(jnp.float32)
    last = place[1] == 1
    x = [own[:, LANES * k : LANES * (k + 1)] for k in range(BLOCKS)]
    for k in range(2):
        closing = [tails[k, pl.ds(place[0] * channels + c, 1), :] for c in range(channels)]
        closing = jnp.concatenate(closing, axis=0)
        x.append(jnp.where(last, closing, after[:, LANES * k : LANES * (k + 1)]))
    row = row_of((channels, LANES))
    lane = lane_of((channels, LANES))
    lag = jnp.zeros((channels, LANES), jnp.int32)
    for c in range(channels):
        lag = jnp.where(row == c, lags[place[0] * channels + c], lag)
    for bit in range(5):
        step = 1 << bit
        turned = [pltpu.roll(v, LANES - step, 1) for v in x]
        moved = (lag & step) != 0
        inside = lane < LANES - step
        x = [
            jnp.where(moved, jnp.where(inside, turned[k], turned[min(k + 1, SPANS)]), x[k])
            for k in range(SPANS + 1)
        ]
    rows[...] = jnp.zeros_like(rows)
    for k in range(SPANS):
        rows[pl.ds(k * channels, channels), :] = mirrored(x[k])
    out[...] = rows[...].astype(jnp.bfloat16)


def align(records, following, record_tail, lag_shift, place):
    channels = records.shape[0]
    held = -(-SPANS * channels // 16) * 16
    vmem = pl.BlockSpec(memory_space=pltpu.VMEM)
    smem = pl.BlockSpec(memory_space=pltpu.SMEM)
    return pl.pallas_call(
        functools.partial(align_kernel, channels),
        out_shape=jax.ShapeDtypeStruct((held, LANES), jnp.bfloat16),
        in_specs=[smem, smem, vmem, vmem, vmem],
        out_specs=vmem,
        scratch_shapes=[
            pltpu.VMEM((2, record_tail.shape[0], LANES), jnp.float32),
            pltpu.VMEM((held, LANES), jnp.float32),
        ],
        name="align",
    )(place, lag_shift, records, following, record_tail)


def parts_of(x):
    first = x.astype(jnp.bfloat16)
    rest = x - first.astype(jnp.float32)
    second = rest.astype(jnp.bfloat16)
    third = (rest - second.astype(jnp.float32)).astype(jnp.bfloat16)
    packed = first.astype(jnp.float32)
    packed = packed + pltpu.roll(second.astype(jnp.float32), RUN, 1)
    packed = packed + pltpu.roll(third.astype(jnp.float32), 2 * RUN, 1)
    return packed.astype(jnp.bfloat16)


def panel_kernel(steps, place, templates, mask, out, wide):
    rows = templates.shape[0]
    width = templates.shape[1]
    room = wide.shape[1]
    wide[:, pl.ds(room - LANES, LANES)] = jnp.zeros((rows, LANES), jnp.bfloat16)
    wide[:, pl.ds(0, width)] = templates[...]
    at = row_of((DEPTH, LANES))
    channel = lane_of((DEPTH, LANES))
    inside = (at >= channel * L) & (at < channel * L + L) & (channel < STEP)
    collect = jnp.where(inside, 1.0, 0.0).astype(jnp.bfloat16)
    part = row_of((LANES, DEPTH))
    column = lane_of((LANES, DEPTH))
    start = (part & (RUN - 1)) * L
    inside = (column >= start) & (column < start + L)
    inside = inside & (part < 3 * RUN) & ((part & (RUN - 1)) < STEP)
    spread = jnp.where(inside, 1.0, 0.0).astype(jnp.bfloat16)
    used = mask[...].astype(jnp.float32).astype(jnp.bfloat16)
    total = mask.shape[1]
    source = row_of((total, LANES))
    target = lane_of((total, LANES))
    for step in range(steps):
        begin = ROWS * step // LANES * LANES
        ahead = ROWS * step - begin
        reach = min(-(-(ahead + ROWS) // LANES) * LANES, room - begin)
        reach = max(reach, DEPTH)
        w = wide[:, pl.ds(begin, reach)].astype(jnp.float32)
        if ahead:
            w = pltpu.roll(w, reach - ahead, 1)
        w = w[:, :DEPTH]
        sums = jnp.dot(w.astype(jnp.bfloat16), collect, preferred_element_type=jnp.float32)
        mean = jnp.dot(parts_of(sums / L), spread, preferred_element_type=jnp.float32)
        u = w - mean
        square = u * u
        high = square.astype(jnp.bfloat16)
        low = (square - high.astype(jnp.float32)).astype(jnp.bfloat16)
        energy = jnp.dot(high, collect, preferred_element_type=jnp.float32)
        energy = energy + jnp.dot(low, collect, preferred_element_type=jnp.float32)
        pick = (source == (place[1] * steps + step) * STEP + target) & (target < STEP)
        pick = jnp.where(pick, 1.0, 0.0).astype(jnp.bfloat16)
        chosen = jnp.dot(used, pick, preferred_element_type=jnp.float32)
        scale = lax.rsqrt(energy + EPSILON) * chosen
        scale = jnp.dot(parts_of(scale), spread, preferred_element_type=jnp.float32)
        out[step] = (u * scale).astype(jnp.bfloat16)


def normalized(templates, channel_mask, place):
    rows, width = templates.shape
    steps = width // ROWS
    block = min(rows, 128)
    room = -(-width // LANES) * LANES
    return pl.pallas_call(
        functools.partial(panel_kernel, steps),
        out_shape=jax.ShapeDtypeStruct((steps, rows, DEPTH), jnp.bfloat16),
        grid=(rows // block,),
        in_specs=[
            pl.BlockSpec(memory_space=pltpu.SMEM),
            pl.BlockSpec((block, width), lambda r: (r, 0)),
            pl.BlockSpec((block, channel_mask.shape[1]), lambda r: (r, 0)),
        ],
        out_specs=pl.BlockSpec((steps, block, DEPTH), lambda r: (0, r, 0)),
        scratch_shapes=[pltpu.VMEM((block, room), jnp.bfloat16)],
        compiler_params=pltpu.CompilerParams(vmem_limit_bytes=40 * 1024 * 1024),
        name="panel",
    )(place, templates, channel_mask)


def prepare(samples, runs, scales, natural_rows, groups):
    at = natural(row_of((3 * LANES, 2 * LANES)))
    to = natural(lane_of((3 * LANES, 2 * LANES)))
    band = (at >= to) & (at < to + L)
    band = jnp.where(band, 1.0, 0.0).astype(jnp.bfloat16)
    lane = lane_of((16, LANES))
    for g in range(groups):
        natural_rows[g, pl.ds(0, samples.shape[1]), :] = samples[g].astype(jnp.float32)
        x = [natural_rows[g, pl.ds(STEP * k, 16), :] for k in range(SPANS)]
        full = jnp.concatenate(x, axis=1)
        square = full * full
        high = square.astype(jnp.bfloat16)
        low = (square - high.astype(jnp.float32)).astype(jnp.bfloat16)
        lhs = jnp.concatenate([full.astype(jnp.bfloat16), high, low], axis=0)
        inverse = []
        for q in range(BLOCKS // 2):
            cut = lhs[:, 2 * LANES * q : 2 * LANES * q + 3 * LANES]
            sums = jnp.dot(cut, band, preferred_element_type=jnp.float32)
            first = sums[0:16]
            second = sums[16:32] + sums[32:48]
            scale = lax.rsqrt(second - first * first / L + L * EPSILON)
            inverse += [scale[:, :LANES], scale[:, LANES:]]
        inverse = swap_runs(inverse)
        z = swap_runs(x[:BLOCKS])
        tail = x[BLOCKS]
        for b in range(BLOCKS):
            scales[g, b] = inverse[b]
            runs[g, b] = z[b]
        for b in range(TILES + 1 - BLOCKS):
            turned = pltpu.roll(tail, LANES - RUN - RUN * b, 1)
            runs[g, BLOCKS + b] = jnp.where(
                lane < LANES - RUN, pltpu.roll(z[b], LANES - RUN, 1), turned
            )


def shifted_rows(runs, g, shifted):
    lane = lane_of((8, LANES)) & (RUN - 1)
    row = row_of((8, LANES))
    early = [pltpu.roll(runs[g, b], LANES - 4, 1) for b in range(TILES)]
    for c in range(STEP):
        offset = c * L % 16
        z = [
            jnp.broadcast_to(runs[g, b, pl.ds(c, 1), :], (8, LANES)) for b in range(TILES + 1)
        ]
        for b in range(TILES):
            halves = []
            for begin in (-offset, 8 - offset):
                move = row + begin
                if begin == -4:
                    here = sheared(jnp.broadcast_to(early[b][c : c + 1], (8, LANES)), 0)
                else:
                    here = sheared(z[b], begin)
                before = after = None
                if begin < 0:
                    before = jnp.where(lane < move + RUN, here, sheared(z[max(b - 1, 0)], begin + RUN))
                if begin + 7 >= 0:
                    after = jnp.where(lane >= move, here, sheared(z[b + 1], begin - RUN))
                if before is None:
                    halves.append(after)
                elif after is None:
                    halves.append(before)
                else:
                    halves.append(jnp.where(move < 0, before, after))
            shifted[c, pl.ds(16 * b, 16), :] = jnp.concatenate(halves, axis=0).astype(jnp.bfloat16)


def hankel_rows(shifted, scales, g, hankel):
    row = row_of((16, LANES))
    for b in range(BLOCKS):
        scale = [
            jnp.broadcast_to(scales[g, b, pl.ds(c, 1), :], (16, LANES)).astype(jnp.bfloat16)
            for c in range(STEP)
        ]

        def tile(c, q):
            return shifted[c, pl.ds(16 * (q - c * L // 16 + b), 16), :] * scale[c]

        for q in range(ROWS // 16):
            c = 16 * q // L
            value = tile(c, q)
            if c + 1 < STEP and 16 * q + 16 > (c + 1) * L:
                value = jnp.where(row < (c + 1) * L - 16 * q, value, tile(c + 1, q))
            hankel[pl.ds(16 * q, 16), pl.ds(LANES * b, LANES)] = value


def product_kernel(
    order, samples, panel_own, panel_other, mask, out,
    runs, scales, natural_rows, shifted, hankel, total, panel, sem,
):
    groups = samples.shape[0]
    half = panel_own.shape[0]
    own = order[groups]
    copy_own = pltpu.make_async_copy(panel_own, panel.at[pl.ds(own * half, half)], sem.at[0])
    copy_other = pltpu.make_async_copy(
        panel_other, panel.at[pl.ds((1 - own) * half, half)], sem.at[1]
    )
    copy_own.start()
    copy_other.start()
    natural_rows[...] = jnp.zeros_like(natural_rows)
    prepare(samples, runs, scales, natural_rows, groups)
    total[...] = jnp.zeros_like(total)
    hankel[pl.ds(ROWS, DEPTH - ROWS), :] = jnp.zeros((DEPTH - ROWS, hankel.shape[1]), jnp.bfloat16)
    copy_own.wait()
    copy_other.wait()

    def step(g, carry):
        shifted_rows(runs, g, shifted)
        hankel_rows(shifted, scales, g, hankel)
        left = panel[order[g]]
        for q in range(BLOCKS // 2):
            cut = pl.ds(2 * LANES * q, 2 * LANES)
            total[:, cut] += jnp.dot(left, hankel[:, cut], preferred_element_type=jnp.float32)
        return carry

    lax.fori_loop(0, groups, step, 0)
    used = jnp.sum(mask[...].astype(jnp.float32), axis=1, keepdims=True)
    weight = jnp.sqrt(L / used)
    height = out.shape[0]
    for r in range(0, height, 32):
        cut = pl.ds(r, 32)
        blocks = swap_runs([total[cut, LANES * b : LANES * (b + 1)] for b in range(BLOCKS)])
        for b in range(BLOCKS):
            out[cut, LANES * b : LANES * (b + 1)] = mirrored(blocks[b]) * weight[r : r + 32]


def product(order, samples, panel_own, panel_other, channel_mask):
    groups = samples.shape[0]
    height = panel_own.shape[1]
    vmem = pl.BlockSpec(memory_space=pltpu.VMEM)
    anywhere = pl.BlockSpec(memory_space=pl.ANY)
    return pl.pallas_call(
        product_kernel,
        out_shape=jax.ShapeDtypeStruct((height, BLOCKS * LANES), jnp.float32),
        in_specs=[pl.BlockSpec(memory_space=pltpu.SMEM), vmem, anywhere, anywhere, vmem],
        out_specs=vmem,
        scratch_shapes=[
            pltpu.VMEM((groups, TILES + 1, 16, LANES), jnp.float32),
            pltpu.VMEM((groups, BLOCKS, 16, LANES), jnp.float32),
            pltpu.VMEM((groups, SPANS * STEP + 4, LANES), jnp.float32),
            pltpu.VMEM((STEP, TILES * 16, LANES), jnp.bfloat16),
            pltpu.VMEM((DEPTH, BLOCKS * LANES), jnp.bfloat16),
            pltpu.VMEM((height, BLOCKS * LANES), jnp.float32),
            pltpu.VMEM((2 * panel_own.shape[0], height, DEPTH), jnp.bfloat16),
            pltpu.SemaphoreType.DMA((2,)),
        ],
        compiler_params=pltpu.CompilerParams(vmem_limit_bytes=48 * 1024 * 1024),
        name="product",
    )(order, samples, panel_own, panel_other, channel_mask)


def per_device(records, record_tail, templates, channel_mask, lag_shift):
    me = lax.axis_index("tmpl")
    devices = lax.axis_size("tmpl")
    core = lax.axis_index("tm")
    cores = lax.axis_size("tm")
    place = jnp.stack([me, core, me]).astype(jnp.int32)
    following = lax.ppermute(records, "tm", [(i + 1, i) for i in range(cores - 1)])
    aligned = align(records, following, record_tail, lag_shift, place)
    own_panel = normalized(templates, channel_mask, place)
    other_panel = lax.ppermute(own_panel, "tm", [(0, 1), (1, 0)])
    channels = records.shape[0]
    groups = lag_shift.shape[0] // STEP
    if channels == STEP and devices & (devices - 1) == 0:
        held = aligned[None]
        reach = 1
        while reach < devices:
            pairs = [(i, i ^ reach) for i in range(devices)]
            held = jnp.concatenate([held, lax.ppermute(held, "tmpl", pairs)], axis=0)
            reach *= 2
        order = jnp.arange(groups, dtype=jnp.int32) ^ me
    else:
        held = lax.all_gather(aligned, "tmpl", axis=0)
        held = held[:, : SPANS * channels].reshape(groups, STEP // channels, SPANS, channels, LANES)
        held = jnp.moveaxis(held, 1, 2).reshape(groups, SPANS * STEP, LANES)
        held = jnp.pad(held, ((0, 0), (0, 4), (0, 0)))
        order = jnp.arange(groups, dtype=jnp.int32)
    order = jnp.concatenate([order, core[None]]).astype(jnp.int32)
    return product(order, held, own_panel, other_panel, channel_mask)


def solution(mesh):
    placed = (P("tmpl", ("win", "tm")), P(None, "win"), P("tmpl", "tm"), P("tmpl", None), P("win"))
    return jax.shard_map(
        per_device, mesh=mesh, in_specs=placed, out_specs=P("tmpl", ("win", "tm")), check_vma=False
    )
```

```python
import functools

import jax
import jax.numpy as jnp
from jax import lax
from jax.experimental import pallas as pl
from jax.experimental.pallas import tpu as pltpu
from jax.sharding import PartitionSpec as P

L = 100
LAGS = 32
EPSILON = 1e-05

LANES = 128
RUN = 16
STEP = 12
ROWS = STEP * L
DEPTH = 1280
BLOCKS = 8
SPANS = 9
TILES = 14


def lane_of(shape):
    return lax.broadcasted_iota(jnp.int32, shape, len(shape) - 1)


def row_of(shape):
    return lax.broadcasted_iota(jnp.int32, shape, 0)


def natural(index):
    return (index & ~(RUN - 1)) + (RUN - 1) - (index & (RUN - 1))


def mirrored(x):
    return jnp.take_along_axis(x, natural(lane_of(x.shape)), axis=1)


def swap_runs(blocks):
    blocks = list(blocks)
    lane = lane_of(blocks[0].shape)
    for bit in range(3):
        step = RUN << bit
        upper = (lane & step) != 0
        for at in range(BLOCKS):
            if at & (1 << bit):
                continue
            low, high = blocks[at], blocks[at | (1 << bit)]
            blocks[at] = jnp.where(upper, pltpu.roll(high, step, 1), low)
            blocks[at | (1 << bit)] = jnp.where(upper, high, pltpu.roll(low, LANES - step, 1))
    return blocks


def sheared(x, first):
    return pltpu.roll(x, first % LANES, 1, stride=1, stride_axis=0)


def align_kernel(channels, place, lags, records, following, tail, out, turned, tails, rows):
    turned[...] = jnp.zeros_like(turned)
    width, count = tail.shape
    turned[pl.ds(0, width), pl.ds(0, count)] = tail[...].astype(jnp.float32)
    for k in range(2):
        tails[k] = turned[pl.ds(LANES * k, LANES), :].T
    own = records[...].astype(jnp.float32)
    after = following[:, : 2 * LANES].astype(jnp.float32)
    last = place[1] == 1
    x = [own[:, LANES * k : LANES * (k + 1)] for k in range(BLOCKS)]
    for k in range(2):
        closing = [tails[k, pl.ds(place[0] * channels + c, 1), :] for c in range(channels)]
        closing = jnp.concatenate(closing, axis=0)
        x.append(jnp.where(last, closing, after[:, LANES * k : LANES * (k + 1)]))
    row = row_of((channels, LANES))
    lane = lane_of((channels, LANES))
    lag = jnp.zeros((channels, LANES), jnp.int32)
    for c in range(channels):
        lag = jnp.where(row == c, lags[place[0] * channels + c], lag)
    for bit in range(5):
        step = 1 << bit
        rolled = [pltpu.roll(v, LANES - step, 1) for v in x]
        moved = (lag & step) != 0
        inside = lane < LANES - step
        x = [
            jnp.where(moved, jnp.where(inside, rolled[k], rolled[min(k + 1, SPANS)]), x[k])
            for k in range(SPANS + 1)
        ]
    rows[...] = jnp.zeros_like(rows)
    for k in range(SPANS):
        rows[pl.ds(k * channels, channels), :] = mirrored(x[k])
    out[...] = rows[...].astype(jnp.bfloat16)


def align(records, following, record_tail, lag_shift, place):
    channels = records.shape[0]
    held = -(-SPANS * channels // 16) * 16
    vmem = pl.BlockSpec(memory_space=pltpu.VMEM)
    smem = pl.BlockSpec(memory_space=pltpu.SMEM)
    return pl.pallas_call(
        functools.partial(align_kernel, channels),
        out_shape=jax.ShapeDtypeStruct((held, LANES), jnp.bfloat16),
        in_specs=[smem, smem, vmem, vmem, vmem],
        out_specs=vmem,
        scratch_shapes=[
            pltpu.VMEM((2 * LANES, LANES), jnp.float32),
            pltpu.VMEM((2, LANES, LANES), jnp.float32),
            pltpu.VMEM((held, LANES), jnp.float32),
        ],
        name="align",
    )(place, lag_shift, records, following, record_tail)


def over_rows(values):
    while len(values) > 1:
        values = [
            values[k] + values[k + 1] if k + 1 < len(values) else values[k]
            for k in range(0, len(values), 2)
        ]
    return jnp.sum(values[0], axis=0, keepdims=True)


def panel_kernel(place, templates, mask, out, chosen, scaled, means):
    count = templates.shape[1]
    second_core = place[1] == 1
    half = mask.shape[0] // 2

    @pl.when(pl.program_id(0) == 0)
    def _():
        used = mask[...].astype(jnp.float32)
        chosen[...] = jnp.where(second_core, used[half:], used[:half])
        scaled[pl.ds(ROWS, DEPTH - ROWS), :] = jnp.zeros((DEPTH - ROWS, count), scaled.dtype)

    row = row_of((8, count))
    middle = L // 8
    tiles = 2 * middle + 1
    first = (place[2] + pl.program_id(0)) * STEP

    def read(pair, t):
        at = pair * 2 * L + 8 * t
        held = templates[pl.ds(at // 16 * 16, 16), :].astype(jnp.float32)
        return held[at % 16 : at % 16 + 8]

    def both(pair, value):
        shared = value(middle)
        early = over_rows([value(t) for t in range(middle)] + [jnp.where(row < 4, shared, 0.0)])
        late = over_rows(
            [jnp.where(row < 4, 0.0, shared)] + [value(t) for t in range(middle + 1, tiles)]
        )
        return early, late

    def pick(values, pair, t):
        a, b = values[2 * pair], values[2 * pair + 1]
        if t == middle:
            return jnp.where(row < 4, a, b)
        return a if t < middle else b

    mean = []
    for pair in range(STEP // 2):
        mean += [v * (1.0 / L) for v in both(pair, lambda t: read(pair, t))]
    scale = []
    for pair in range(STEP // 2):

        def squared(t):
            u = read(pair, t) - pick(mean, pair, t)
            scaled[pl.ds(pair * 2 * L + 8 * t, 8), :] = u
            return u * u

        energies = both(pair, squared)
        for c in range(2):
            used = chosen[pl.ds(first + 2 * pair + c, 1), :]
            scale.append(lax.rsqrt(energies[c] + EPSILON) * used)
    for pair in range(STEP // 2):
        for t in range(tiles):
            at = pl.ds(pair * 2 * L + 8 * t, 8)
            scaled[at, :] = scaled[at, :] * pick(scale, pair, t)
    for k in range(DEPTH // LANES):
        part = scaled[pl.ds(LANES * k, LANES), :].astype(jnp.bfloat16)
        out[0, :, pl.ds(LANES * k, LANES)] = part.T


def normalized(templates, channel_mask, place, begin, steps):
    width, rows = templates.shape
    place = jnp.concatenate([place, jnp.full((1,), begin, jnp.int32)])
    return pl.pallas_call(
        panel_kernel,
        out_shape=jax.ShapeDtypeStruct((steps, rows, DEPTH), jnp.bfloat16),
        grid=(steps,),
        in_specs=[
            pl.BlockSpec(memory_space=pltpu.SMEM),
            pl.BlockSpec((ROWS, rows), lambda i: (i + begin, 0)),
            pl.BlockSpec(memory_space=pltpu.VMEM),
        ],
        out_specs=pl.BlockSpec((1, rows, DEPTH), lambda i: (i, 0, 0)),
        scratch_shapes=[
            pltpu.VMEM((channel_mask.shape[0] // 2, rows), jnp.float32),
            pltpu.VMEM((DEPTH, rows), jnp.float32),
            pltpu.VMEM((16, rows), jnp.float32),
        ],
        compiler_params=pltpu.CompilerParams(vmem_limit_bytes=24 * 1024 * 1024),
        cost_estimate=pl.CostEstimate(flops=10**9, bytes_accessed=5 * 10**6, transcendentals=0),
        name="panel",
    )(place, templates, channel_mask)


def prepare(samples, runs, scales, staged, left, spread, groups):
    at = natural(row_of((3 * LANES, 2 * LANES)))
    to = natural(lane_of((3 * LANES, 2 * LANES)))
    band = (at >= to) & (at < to + L)
    band = jnp.where(band, 1.0, 0.0).astype(jnp.bfloat16)
    rows = 16 * groups
    lane = lane_of((16, LANES))
    for g in range(groups):
        staged[g] = samples[g].astype(jnp.float32)
    for g in range(groups):
        for k in range(SPANS):
            x = staged[g, pl.ds(min(STEP * k, SPANS * STEP + 4 - 16), 16), :]
            cut = pl.ds(LANES * k, LANES)
            square = x * x
            high = square.astype(jnp.bfloat16)
            left[pl.ds(16 * g, 16), cut] = x.astype(jnp.bfloat16)
            left[pl.ds(rows + 16 * g, 16), cut] = high
            low = square - high.astype(jnp.float32)
            left[pl.ds(2 * rows + 16 * g, 16), cut] = low.astype(jnp.bfloat16)
    for q in range(BLOCKS // 2):
        cut = left[:, pl.ds(2 * LANES * q, 3 * LANES)]
        sums = jnp.dot(cut, band, preferred_element_type=jnp.float32)
        first = sums[:rows]
        second = sums[rows : 2 * rows] + sums[2 * rows :]
        scale = lax.rsqrt(second - first * first / L + L * EPSILON)
        spread[2 * q] = scale[:, :LANES]
        spread[2 * q + 1] = scale[:, LANES:]
    for g in range(groups):
        inverse = swap_runs([spread[b, pl.ds(16 * g, 16), :] for b in range(BLOCKS)])
        x = [staged[g, pl.ds(STEP * k, 16), :] for k in range(BLOCKS)]
        tail = staged[g, pl.ds(STEP * BLOCKS, 16), :]
        z = swap_runs(x)
        for b in range(BLOCKS):
            scales[g, b] = inverse[b]
            runs[g, b] = z[b]
        for b in range(TILES + 1 - BLOCKS):
            turned = pltpu.roll(tail, LANES - RUN - RUN * b, 1)
            runs[g, BLOCKS + b] = jnp.where(
                lane < LANES - RUN, pltpu.roll(z[b], LANES - RUN, 1), turned
            )


def shifted_rows(runs, g, shifted):
    lane = lane_of((8, LANES)) & (RUN - 1)
    row = row_of((8, LANES))
    early = [pltpu.roll(runs[g, b], LANES - 4, 1) for b in range(TILES)]
    for c in range(STEP):
        offset = c * L % 16
        z = [
            jnp.broadcast_to(runs[g, b, pl.ds(c, 1), :], (8, LANES)) for b in range(TILES + 1)
        ]
        for b in range(TILES):
            halves = []
            for begin in (-offset, 8 - offset):
                move = row + begin
                if begin == -4:
                    here = sheared(jnp.broadcast_to(early[b][c : c + 1], (8, LANES)), 0)
                else:
                    here = sheared(z[b], begin)
                before = after = None
                if begin < 0:
                    before = jnp.where(lane < move + RUN, here, sheared(z[max(b - 1, 0)], begin + RUN))
                if begin + 7 >= 0:
                    after = jnp.where(lane >= move, here, sheared(z[b + 1], begin - RUN))
                if before is None:
                    halves.append(after)
                elif after is None:
                    halves.append(before)
                else:
                    halves.append(jnp.where(move < 0, before, after))
            shifted[c, pl.ds(16 * b, 16), :] = jnp.concatenate(halves, axis=0).astype(jnp.bfloat16)


def hankel_rows(shifted, scales, g, hankel):
    row = row_of((16, LANES))
    for b in range(BLOCKS):
        scale = [
            jnp.broadcast_to(scales[g, b, pl.ds(c, 1), :], (16, LANES)).astype(jnp.bfloat16)
            for c in range(STEP)
        ]

        def tile(c, q):
            return shifted[c, pl.ds(16 * (q - c * L // 16 + b), 16), :] * scale[c]

        for q in range(ROWS // 16):
            c = 16 * q // L
            value = tile(c, q)
            if c + 1 < STEP and 16 * q + 16 > (c + 1) * L:
                value = jnp.where(row < (c + 1) * L - 16 * q, value, tile(c + 1, q))
            hankel[pl.ds(16 * q, 16), pl.ds(LANES * b, LANES)] = value


def product_kernel(closing, parts, begin, half, order, samples, *rest):
    panels = rest[: 2 * parts]
    rest = rest[2 * parts :]
    if closing:
        mask, before, out = rest[:3]
        total, staging, sem = rest[-3:]
        rest = rest[3:-3]
    else:
        total = rest[0]
        rest = rest[1:]
    runs, scales, staged, left, spread, shifted, hankel_a, hankel_b = rest
    groups = samples.shape[0]
    prepare(samples, runs, scales, staged, left, spread, groups)
    hankels = (hankel_a, hankel_b)
    for hankel in hankels:
        hankel[pl.ds(ROWS, DEPTH - ROWS), :] = jnp.zeros(
            (DEPTH - ROWS, hankel.shape[1]), jnp.bfloat16
        )

    def fill(g, hankel):
        shifted_rows(runs, g, shifted)
        hankel_rows(shifted, scales, g, hankel)

    def panel(g):
        slot = (begin + g) ^ order[0]
        own = slot // half == order[1]
        at = slot % half
        each = half // parts
        mine, theirs = panels[0][at % each], panels[parts][at % each]
        for k in range(1, parts):
            mine = jnp.where(at // each == k, panels[k][at % each], mine)
            theirs = jnp.where(at // each == k, panels[parts + k][at % each], theirs)
        return jnp.where(own, mine, theirs)

    fill(0, hankel_a)
    for g in range(groups):
        if g + 1 < groups:
            fill(g + 1, hankels[(g + 1) % 2])
        held = panel(g)
        for q in range(BLOCKS // 2):
            cut = pl.ds(2 * LANES * q, 2 * LANES)
            value = jnp.dot(held, hankels[g % 2][:, cut], preferred_element_type=jnp.float32)
            if g:
                total[:, cut] += value
            elif closing:
                total[:, cut] = before[:, cut] + value
            else:
                total[:, cut] = value
    if not closing:
        return
    height = out.shape[0]
    used = jnp.sum(mask[...].astype(jnp.float32), axis=0, keepdims=True)
    weight = jnp.broadcast_to(jnp.sqrt(L / used), (LANES, height)).T
    size = 32
    copies = []
    for r in range(0, height, 8):
        cut = pl.ds(r, 8)
        blocks = swap_runs([total[cut, LANES * b : LANES * (b + 1)] for b in range(BLOCKS)])
        for b in range(BLOCKS):
            staging[cut, LANES * b : LANES * (b + 1)] = mirrored(blocks[b]) * weight[r : r + 8]
        if (r + 8) % size == 0:
            rows = pl.ds(r + 8 - size, size)
            copies.append(
                pltpu.make_async_copy(staging.at[rows], out.at[rows], sem.at[len(copies)])
            )
            copies[-1].start()
    for copy in copies:
        copy.wait()


def product(order, samples, panels, begin, closing=None):
    groups = samples.shape[0]
    height = panels[0].shape[1]
    half = sum(panel.shape[0] for panel in panels) // 2
    vmem = pl.BlockSpec(memory_space=pltpu.VMEM)
    held = SPANS * STEP + 4
    extra = () if closing is None else closing
    scratch = [
        pltpu.VMEM((groups, TILES + 1, 16, LANES), jnp.float32),
        pltpu.VMEM((groups, BLOCKS, 16, LANES), jnp.float32),
        pltpu.VMEM((groups, held, LANES), jnp.float32),
        pltpu.VMEM((3 * 16 * groups, SPANS * LANES), jnp.bfloat16),
        pltpu.VMEM((BLOCKS, 16 * groups, LANES), jnp.float32),
        pltpu.VMEM((STEP, TILES * 16, LANES), jnp.bfloat16),
        pltpu.VMEM((DEPTH, BLOCKS * LANES), jnp.bfloat16),
        pltpu.VMEM((DEPTH, BLOCKS * LANES), jnp.bfloat16),
    ]
    if closing is not None:
        scratch += [
            pltpu.VMEM((height, BLOCKS * LANES), jnp.float32),
            pltpu.VMEM((height, BLOCKS * LANES), jnp.float32),
            pltpu.SemaphoreType.DMA((height // 32,)),
        ]
    return pl.pallas_call(
        functools.partial(
            product_kernel, closing is not None, len(panels) // 2, begin, half
        ),
        out_shape=jax.ShapeDtypeStruct((height, BLOCKS * LANES), jnp.float32),
        in_specs=[pl.BlockSpec(memory_space=pltpu.SMEM)] + [vmem] * (1 + len(panels) + len(extra)),
        out_specs=vmem if closing is None else pl.BlockSpec(memory_space=pl.ANY),
        scratch_shapes=scratch,
        compiler_params=pltpu.CompilerParams(vmem_limit_bytes=20 * 1024 * 1024),
        cost_estimate=pl.CostEstimate(
            flops=2 * height * groups * ROWS * BLOCKS * LANES,
            bytes_accessed=2 * groups * height * DEPTH + 4 * height * BLOCKS * LANES,
            transcendentals=0,
        ),
        name="product",
    )(order, samples, *panels, *extra)


def per_device(records, record_tail, templates, channel_mask, lag_shift):
    me = lax.axis_index("tmpl")
    devices = lax.axis_size("tmpl")
    core = lax.axis_index("tm")
    cores = lax.axis_size("tm")
    channels = records.shape[0]
    groups = lag_shift.shape[0] // STEP
    half = groups // cores
    place = jnp.stack([me, core]).astype(jnp.int32)
    templates = templates.T
    channel_mask = channel_mask.T
    pairs = [(0, 1), (1, 0)]
    following = lax.ppermute(records, "tm", [(i + 1, i) for i in range(cores - 1)])
    early = normalized(templates, channel_mask, place, 0, half // 2)
    early_other = lax.ppermute(early, "tm", pairs)
    following, early = lax.optimization_barrier((following, early))
    aligned = align(records, following, record_tail.T, lag_shift, place)
    templates, aligned = lax.optimization_barrier((templates, aligned))
    late = normalized(templates, channel_mask, place, half // 2, half - half // 2)
    late_other = lax.ppermute(late, "tm", pairs)
    if channels == STEP and devices & (devices - 1) == 0:
        held = aligned[None]
        received = held
        reach = 1
        while reach < devices:
            if reach > 1:
                held = jnp.concatenate([held, received], axis=0)
            received = lax.ppermute(held, "tmpl", [(i, i ^ reach) for i in range(devices)])
            reach *= 2
        near, far = held, received
        order = place
    else:
        held = lax.all_gather(aligned, "tmpl", axis=0)
        held = held[:, : SPANS * channels].reshape(groups, STEP // channels, SPANS, channels, LANES)
        held = jnp.moveaxis(held, 1, 2).reshape(groups, SPANS * STEP, LANES)
        held = jnp.pad(held, ((0, 0), (0, 4), (0, 0)))
        near, far = held[:half], held[half:]
        order = place * jnp.array([0, 1], jnp.int32)
    panels = (early, late, early_other, late_other)

    total = product(order, near, panels, 0)
    return product(order, far, panels, half, (channel_mask, total))


def solution(mesh):
    placed = (P("tmpl", ("win", "tm")), P(None, "win"), P("tmpl", "tm"), P("tmpl", None), P("win"))
    return jax.shard_map(
        per_device, mesh=mesh, in_specs=placed, out_specs=P("tmpl", ("win", "tm")), check_vma=False
    )
```

```python
import functools

import jax
import jax.numpy as jnp
from jax import lax
from jax.experimental import pallas as pl
from jax.experimental.pallas import tpu as pltpu
from jax.sharding import PartitionSpec as P

L = 100
LAGS = 32
EPSILON = 1e-05

LANES = 128
RUN = 16
STEP = 12
ROWS = STEP * L
DEPTH = 1280
BLOCKS = 8
SPANS = 9
TILES = 14


def lane_of(shape):
    return lax.broadcasted_iota(jnp.int32, shape, len(shape) - 1)


def row_of(shape):
    return lax.broadcasted_iota(jnp.int32, shape, 0)


def natural(index):
    return (index & ~(RUN - 1)) + (RUN - 1) - (index & (RUN - 1))


def mirrored(x):
    return jnp.take_along_axis(x, natural(lane_of(x.shape)), axis=1)


def swap_runs(blocks):
    blocks = list(blocks)
    lane = lane_of(blocks[0].shape)
    for bit in range(3):
        step = RUN << bit
        upper = (lane & step) != 0
        for at in range(BLOCKS):
            if at & (1 << bit):
                continue
            low, high = blocks[at], blocks[at | (1 << bit)]
            blocks[at] = jnp.where(upper, pltpu.roll(high, step, 1), low)
            blocks[at | (1 << bit)] = jnp.where(upper, high, pltpu.roll(low, LANES - step, 1))
    return blocks


def sheared(x, first):
    return pltpu.roll(x, first % LANES, 1, stride=1, stride_axis=0)


def stage_kernel(channels, place, lags, tail, closing, lag, turned, tails):
    turned[...] = jnp.zeros_like(turned)
    width, count = tail.shape
    turned[pl.ds(0, width), pl.ds(0, count)] = tail[...].astype(jnp.float32)
    for k in range(2):
        tails[k] = turned[pl.ds(LANES * k, LANES), :].T
    for k in range(2):
        for c in range(channels):
            row = tails[k, pl.ds(place[0] * channels + c, 1), :]
            closing[pl.ds(c, 1), pl.ds(k * LANES, LANES)] = row
    row = row_of((channels, LANES))
    moves = jnp.zeros((channels, LANES), jnp.int32)
    for c in range(channels):
        moves = jnp.where(row == c, lags[place[0] * channels + c], moves)
    lag[...] = moves


def stage(channels, record_tail, lag_shift, place):
    vmem = pl.BlockSpec(memory_space=pltpu.VMEM)
    smem = pl.BlockSpec(memory_space=pltpu.SMEM)
    return pl.pallas_call(
        functools.partial(stage_kernel, channels),
        out_shape=(
            jax.ShapeDtypeStruct((channels, 2 * LANES), jnp.float32),
            jax.ShapeDtypeStruct((channels, LANES), jnp.int32),
        ),
        in_specs=[smem, smem, vmem],
        out_specs=(vmem, vmem),
        scratch_shapes=[
            pltpu.VMEM((2 * LANES, LANES), jnp.float32),
            pltpu.VMEM((2, LANES, LANES), jnp.float32),
        ],
        compiler_params=pltpu.CompilerParams(vmem_limit_bytes=4 * 1024 * 1024),
        cost_estimate=pl.CostEstimate(flops=3 * 10**9, bytes_accessed=10**6, transcendentals=0),
        name="stage",
    )(place, lag_shift, record_tail)


def align_kernel(channels, place, records, following, closing, lag, out, rows):
    rows[...] = jnp.zeros_like(rows)
    last = place[1] == 1
    own = records[...].astype(jnp.float32)
    after = following[:, : 2 * LANES].astype(jnp.float32)
    after = jnp.where(last, closing[...], after)
    x = [own[:, LANES * k : LANES * (k + 1)] for k in range(BLOCKS)]
    x += [after[:, :LANES], after[:, LANES:]]
    lane = lane_of((channels, LANES))
    for bit in range(5):
        step = 1 << bit
        rolled = [pltpu.roll(v, LANES - step, 1) for v in x]
        moved = (lag[...] & step) != 0
        inside = lane < LANES - step
        x = [
            jnp.where(moved, jnp.where(inside, rolled[k], rolled[min(k + 1, SPANS)]), x[k])
            for k in range(SPANS + 1)
        ]
    for k in range(SPANS):
        rows[pl.ds(k * channels, channels), :] = mirrored(x[k])
    out[...] = rows[...].astype(jnp.bfloat16)


def align(records, following, closing, lag, place):
    channels = records.shape[0]
    held = -(-SPANS * channels // 16) * 16
    vmem = pl.BlockSpec(memory_space=pltpu.VMEM)
    smem = pl.BlockSpec(memory_space=pltpu.SMEM)
    return pl.pallas_call(
        functools.partial(align_kernel, channels),
        out_shape=jax.ShapeDtypeStruct((held, LANES), jnp.bfloat16),
        in_specs=[smem, vmem, vmem, vmem, vmem],
        out_specs=vmem,
        scratch_shapes=[pltpu.VMEM((held, LANES), jnp.float32)],
        compiler_params=pltpu.CompilerParams(vmem_limit_bytes=4 * 1024 * 1024),
        cost_estimate=pl.CostEstimate(flops=3 * 10**9, bytes_accessed=10**6, transcendentals=0),
        name="align",
    )(place, records, following, closing, lag)


def over_rows(values):
    while len(values) > 1:
        values = [
            values[k] + values[k + 1] if k + 1 < len(values) else values[k]
            for k in range(0, len(values), 2)
        ]
    return jnp.sum(values[0], axis=0, keepdims=True)


def panel_kernel(begin, steps, place, templates, mask, out, weight, chosen, scaled):
    count = templates.shape[1]

    @pl.when(pl.program_id(0) == 0)
    def _():
        half = mask.shape[0] // 2
        used = mask[...].astype(jnp.float32)
        chosen[...] = jnp.where(place[1] == 1, used[half:], used[:half])
        scale = jnp.sqrt(L / jnp.sum(used, axis=0, keepdims=True))
        weight[...] = jnp.broadcast_to(scale, (LANES, count)).T
        scaled[pl.ds(ROWS, DEPTH - ROWS), :] = jnp.zeros((DEPTH - ROWS, count), scaled.dtype)

    row = row_of((8, count))
    middle = L // 8
    tiles = 2 * middle + 1
    first = ((begin + pl.program_id(0)) ^ (place[0] % steps)) * STEP

    def read(pair, t):
        at = pair * 2 * L + 8 * t
        held = templates[pl.ds(at // 16 * 16, 16), :].astype(jnp.float32)
        return held[at % 16 : at % 16 + 8]

    def both(pair, value):
        shared = value(middle)
        early = over_rows([value(t) for t in range(middle)] + [jnp.where(row < 4, shared, 0.0)])
        late = over_rows(
            [jnp.where(row < 4, 0.0, shared)] + [value(t) for t in range(middle + 1, tiles)]
        )
        return early, late

    def pick(values, pair, t):
        a, b = values[2 * pair], values[2 * pair + 1]
        if t == middle:
            return jnp.where(row < 4, a, b)
        return a if t < middle else b

    mean = []
    for pair in range(STEP // 2):
        mean += [v * (1.0 / L) for v in both(pair, lambda t: read(pair, t))]
    scale = []
    for pair in range(STEP // 2):

        def squared(t):
            u = read(pair, t) - pick(mean, pair, t)
            scaled[pl.ds(pair * 2 * L + 8 * t, 8), :] = u
            return u * u

        energies = both(pair, squared)
        for c in range(2):
            used = chosen[pl.ds(first + 2 * pair + c, 1), :]
            scale.append(lax.rsqrt(energies[c] + EPSILON) * used)
    for pair in range(STEP // 2):
        for t in range(tiles):
            at = pl.ds(pair * 2 * L + 8 * t, 8)
            scaled[at, :] = scaled[at, :] * pick(scale, pair, t)
    for k in range(DEPTH // LANES):
        part = scaled[pl.ds(LANES * k, LANES), :].astype(jnp.bfloat16)
        out[0, :, pl.ds(LANES * k, LANES)] = part.T


def normalized(templates, channel_mask, place, begin, steps):
    width, rows = templates.shape
    every = width // ROWS
    return pl.pallas_call(
        functools.partial(panel_kernel, begin, every),
        out_shape=(
            jax.ShapeDtypeStruct((steps, rows, DEPTH), jnp.bfloat16),
            jax.ShapeDtypeStruct((rows, LANES), jnp.float32),
        ),
        grid_spec=pltpu.PrefetchScalarGridSpec(
            num_scalar_prefetch=1,
            grid=(steps,),
            in_specs=[
                pl.BlockSpec((ROWS, rows), lambda i, at: ((i + begin) ^ (at[0] % every), 0)),
                pl.BlockSpec(memory_space=pltpu.VMEM),
            ],
            out_specs=(
                pl.BlockSpec((1, rows, DEPTH), lambda i, at: (i, 0, 0)),
                pl.BlockSpec((rows, LANES), lambda i, at: (0, 0)),
            ),
            scratch_shapes=[
                pltpu.VMEM((channel_mask.shape[0] // 2, rows), jnp.float32),
                pltpu.VMEM((DEPTH, rows), jnp.float32),
            ],
        ),
        compiler_params=pltpu.CompilerParams(vmem_limit_bytes=24 * 1024 * 1024),
        cost_estimate=pl.CostEstimate(
            flops=2 * 10**9, bytes_accessed=3 * 10**6, transcendentals=0
        ),
        name="panel",
    )(place, templates, channel_mask)


def prepare(samples, runs, scales, staged, left, spread, groups):
    at = natural(row_of((3 * LANES, 2 * LANES)))
    to = natural(lane_of((3 * LANES, 2 * LANES)))
    band = (at >= to) & (at < to + L)
    band = jnp.where(band, 1.0, 0.0).astype(jnp.bfloat16)
    rows = 16 * groups
    lane = lane_of((16, LANES))
    for g in range(groups):
        staged[g] = samples[g].astype(jnp.float32)
    for g in range(groups):
        for k in range(SPANS):
            x = staged[g, pl.ds(min(STEP * k, SPANS * STEP + 4 - 16), 16), :]
            cut = pl.ds(LANES * k, LANES)
            square = x * x
            high = square.astype(jnp.bfloat16)
            left[pl.ds(16 * g, 16), cut] = x.astype(jnp.bfloat16)
            left[pl.ds(rows + 16 * g, 16), cut] = high
            low = square - high.astype(jnp.float32)
            left[pl.ds(2 * rows + 16 * g, 16), cut] = low.astype(jnp.bfloat16)
    for q in range(BLOCKS // 2):
        cut = left[:, pl.ds(2 * LANES * q, 3 * LANES)]
        sums = jnp.dot(cut, band, preferred_element_type=jnp.float32)
        first = sums[:rows]
        second = sums[rows : 2 * rows] + sums[2 * rows :]
        scale = lax.rsqrt(second - first * first / L + L * EPSILON)
        spread[2 * q] = scale[:, :LANES]
        spread[2 * q + 1] = scale[:, LANES:]
    for g in range(groups):
        inverse = swap_runs([spread[b, pl.ds(16 * g, 16), :] for b in range(BLOCKS)])
        x = [staged[g, pl.ds(STEP * k, 16), :] for k in range(BLOCKS)]
        tail = staged[g, pl.ds(STEP * BLOCKS, 16), :]
        z = swap_runs(x)
        for b in range(BLOCKS):
            scales[g, b] = inverse[b]
            runs[g, b] = z[b]
        for b in range(TILES + 1 - BLOCKS):
            turned = pltpu.roll(tail, LANES - RUN - RUN * b, 1)
            runs[g, BLOCKS + b] = jnp.where(
                lane < LANES - RUN, pltpu.roll(z[b], LANES - RUN, 1), turned
            )


def shifted_rows(runs, g, shifted):
    lane = lane_of((8, LANES)) & (RUN - 1)
    row = row_of((8, LANES))
    early = [pltpu.roll(runs[g, b], LANES - 4, 1) for b in range(TILES)]
    for c in range(STEP):
        offset = c * L % 16
        z = [
            jnp.broadcast_to(runs[g, b, pl.ds(c, 1), :], (8, LANES)) for b in range(TILES + 1)
        ]
        for b in range(TILES):
            halves = []
            for begin in (-offset, 8 - offset):
                move = row + begin
                if begin == -4:
                    here = sheared(jnp.broadcast_to(early[b][c : c + 1], (8, LANES)), 0)
                else:
                    here = sheared(z[b], begin)
                before = after = None
                if begin < 0:
                    before = jnp.where(lane < move + RUN, here, sheared(z[max(b - 1, 0)], begin + RUN))
                if begin + 7 >= 0:
                    after = jnp.where(lane >= move, here, sheared(z[b + 1], begin - RUN))
                if before is None:
                    halves.append(after)
                elif after is None:
                    halves.append(before)
                else:
                    halves.append(jnp.where(move < 0, before, after))
            shifted[c, pl.ds(16 * b, 16), :] = jnp.concatenate(halves, axis=0).astype(jnp.bfloat16)


def hankel_rows(shifted, scales, g, hankel):
    row = row_of((16, LANES))
    for b in range(BLOCKS):
        scale = [
            jnp.broadcast_to(scales[g, b, pl.ds(c, 1), :], (16, LANES)).astype(jnp.bfloat16)
            for c in range(STEP)
        ]

        def tile(c, q):
            return shifted[c, pl.ds(16 * (q - c * L // 16 + b), 16), :] * scale[c]

        for q in range(ROWS // 16):
            c = 16 * q // L
            value = tile(c, q)
            if c + 1 < STEP and 16 * q + 16 > (c + 1) * L:
                value = jnp.where(row < (c + 1) * L - 16 * q, value, tile(c + 1, q))
            hankel[pl.ds(16 * q, 16), pl.ds(LANES * b, LANES)] = value


def product_kernel(closing, parts, begin, half, order, samples, *rest):
    panels = rest[: 2 * parts]
    rest = rest[2 * parts :]
    if closing:
        weight, before, out = rest[:3]
        total, staging, sem = rest[-3:]
        rest = rest[3:-3]
    else:
        total = rest[0]
        rest = rest[1:]
    runs, scales, staged, left, spread, shifted, hankel_a, hankel_b = rest
    groups = samples.shape[0]
    prepare(samples, runs, scales, staged, left, spread, groups)
    hankels = (hankel_a, hankel_b)
    for hankel in hankels:
        hankel[pl.ds(ROWS, DEPTH - ROWS), :] = jnp.zeros(
            (DEPTH - ROWS, hankel.shape[1]), jnp.bfloat16
        )

    def fill(g, hankel):
        shifted_rows(runs, g, shifted)
        hankel_rows(shifted, scales, g, hankel)

    own = ((begin ^ order[0]) // half) == order[1]

    def panel(g):
        each = half // parts
        return jnp.where(own, panels[g // each][g % each], panels[parts + g // each][g % each])

    fill(0, hankel_a)
    for g in range(groups):
        if g + 1 < groups:
            fill(g + 1, hankels[(g + 1) % 2])
        held = panel(g)
        for q in range(BLOCKS // 2):
            cut = pl.ds(2 * LANES * q, 2 * LANES)
            value = jnp.dot(held, hankels[g % 2][:, cut], preferred_element_type=jnp.float32)
            if g:
                total[:, cut] += value
            elif closing:
                total[:, cut] = before[:, cut] + value
            else:
                total[:, cut] = value
    if not closing:
        return
    height = out.shape[0]
    size = 32
    copies = []
    for r in range(0, height, 8):
        cut = pl.ds(r, 8)
        blocks = swap_runs([total[cut, LANES * b : LANES * (b + 1)] for b in range(BLOCKS)])
        for b in range(BLOCKS):
            staging[cut, LANES * b : LANES * (b + 1)] = mirrored(blocks[b]) * weight[cut, :]
        if (r + 8) % size == 0:
            rows = pl.ds(r + 8 - size, size)
            copies.append(
                pltpu.make_async_copy(staging.at[rows], out.at[rows], sem.at[len(copies)])
            )
            copies[-1].start()
    for copy in copies:
        copy.wait()


def product(order, samples, panels, begin, closing=None):
    groups = samples.shape[0]
    height = panels[0].shape[1]
    half = sum(panel.shape[0] for panel in panels) // 2
    vmem = pl.BlockSpec(memory_space=pltpu.VMEM)
    held = SPANS * STEP + 4
    extra = () if closing is None else closing
    scratch = [
        pltpu.VMEM((groups, TILES + 1, 16, LANES), jnp.float32),
        pltpu.VMEM((groups, BLOCKS, 16, LANES), jnp.float32),
        pltpu.VMEM((groups, held, LANES), jnp.float32),
        pltpu.VMEM((3 * 16 * groups, SPANS * LANES), jnp.bfloat16),
        pltpu.VMEM((BLOCKS, 16 * groups, LANES), jnp.float32),
        pltpu.VMEM((STEP, TILES * 16, LANES), jnp.bfloat16),
        pltpu.VMEM((DEPTH, BLOCKS * LANES), jnp.bfloat16),
        pltpu.VMEM((DEPTH, BLOCKS * LANES), jnp.bfloat16),
    ]
    if closing is not None:
        scratch += [
            pltpu.VMEM((height, BLOCKS * LANES), jnp.float32),
            pltpu.VMEM((height, BLOCKS * LANES), jnp.float32),
            pltpu.SemaphoreType.DMA((height // 32,)),
        ]
    return pl.pallas_call(
        functools.partial(
            product_kernel, closing is not None, len(panels) // 2, begin, half
        ),
        out_shape=jax.ShapeDtypeStruct((height, BLOCKS * LANES), jnp.float32),
        in_specs=[pl.BlockSpec(memory_space=pltpu.SMEM)] + [vmem] * (1 + len(panels) + len(extra)),
        out_specs=vmem if closing is None else pl.BlockSpec(memory_space=pl.ANY),
        scratch_shapes=scratch,
        compiler_params=pltpu.CompilerParams(vmem_limit_bytes=20 * 1024 * 1024),
        cost_estimate=pl.CostEstimate(
            flops=2 * height * groups * ROWS * BLOCKS * LANES,
            bytes_accessed=2 * groups * height * DEPTH + 4 * height * BLOCKS * LANES,
            transcendentals=0,
        ),
        name="product",
    )(order, samples, *panels, *extra)


def per_device(records, record_tail, templates, channel_mask, lag_shift):
    me = lax.axis_index("tmpl")
    devices = lax.axis_size("tmpl")
    core = lax.axis_index("tm")
    cores = lax.axis_size("tm")
    channels = records.shape[0]
    groups = lag_shift.shape[0] // STEP
    half = groups // cores
    place = jnp.stack([me, core]).astype(jnp.int32)
    templates = templates.T
    channel_mask = channel_mask.T
    pairs = [(0, 1), (1, 0)]
    following = lax.ppermute(records, "tm", [(i + 1, i) for i in range(cores - 1)])
    closing, lag = stage(channels, record_tail.T, lag_shift, place)
    aligned = align(records, following, closing, lag, place)
    doubling = channels == STEP and devices & (devices - 1) == 0
    ahead = (0, half // 2)
    parts = []
    held = received = aligned[None]
    reach = 1
    order = place if doubling else place * jnp.array([0, 1], jnp.int32)
    begun, received = lax.optimization_barrier((order, received))
    while reach < devices:
        if doubling:
            if reach > 1:
                held = jnp.concatenate([held, received], axis=0)
            received = lax.ppermute(held, "tmpl", [(i, i ^ reach) for i in range(devices)])
        if len(parts) < 2:
            part, weight = normalized(templates, channel_mask, begun, ahead[len(parts)], half // 2)
            part, received, begun = lax.optimization_barrier((part, received, begun))
            parts.append(part)
        reach *= 2
    panels = parts + [lax.ppermute(part, "tm", pairs) for part in parts]
    if doubling:
        near, far = held, received
    else:
        held = lax.all_gather(aligned, "tmpl", axis=0)
        held = held[:, : SPANS * channels].reshape(groups, STEP // channels, SPANS, channels, LANES)
        held = jnp.moveaxis(held, 1, 2).reshape(groups, SPANS * STEP, LANES)
        held = jnp.pad(held, ((0, 0), (0, 4), (0, 0)))
        near, far = held[:half], held[half:]
    total = product(order, near, panels, 0)
    return product(order, far, panels, half, (weight, total))


def solution(mesh):
    placed = (P("tmpl", ("win", "tm")), P(None, "win"), P("tmpl", "tm"), P("tmpl", None), P("win"))
    return jax.shard_map(
        per_device, mesh=mesh, in_specs=placed, out_specs=P("tmpl", ("win", "tm")), check_vma=False
    )
```

```python
import functools

import jax
import jax.numpy as jnp
from jax import lax
from jax.experimental import pallas as pl
from jax.experimental.pallas import tpu as pltpu
from jax.sharding import PartitionSpec as P

L = 100
LAGS = 32
EPSILON = 1e-05

LANES = 128
RUN = 16
STEP = 12
ROWS = STEP * L
DEPTH = 1280
BLOCKS = 8
SPANS = 9
TILES = 14


def lane_of(shape):
    return lax.broadcasted_iota(jnp.int32, shape, len(shape) - 1)


def row_of(shape):
    return lax.broadcasted_iota(jnp.int32, shape, 0)


def natural(index):
    return (index & ~(RUN - 1)) + (RUN - 1) - (index & (RUN - 1))


def mirrored(x):
    return jnp.take_along_axis(x, natural(lane_of(x.shape)), axis=1)


def turned_runs(x, by):
    by = by % BLOCKS
    return pltpu.roll(x, RUN * by, 1) if by else x


def swap_runs(blocks, mirror=False):
    lane = lane_of(blocks[0].shape)
    held = []
    for k in range(BLOCKS):
        by = -k % BLOCKS
        x = blocks[by]
        if mirror:
            source = natural((lane - RUN * by) & (LANES - 1))
            held.append(jnp.take_along_axis(x, source, axis=1))
        else:
            held.append(turned_runs(x, by))
    for bit in range(3):
        taken = (lane & (RUN << bit)) != 0
        held = [jnp.where(taken, held[(k - (1 << bit)) % BLOCKS], held[k]) for k in range(BLOCKS)]
    return [turned_runs(held[k], -k) for k in range(BLOCKS)]


def sheared(x, first):
    return pltpu.roll(x, first % LANES, 1, stride=1, stride_axis=0)


def stage_kernel(channels, place, lags, tail, closing, lag, turned, tails):
    turned[...] = jnp.zeros_like(turned)
    width, count = tail.shape
    turned[pl.ds(0, width), pl.ds(0, count)] = tail[...].astype(jnp.float32)
    for k in range(2):
        tails[k] = turned[pl.ds(LANES * k, LANES), :].T
    for k in range(2):
        for c in range(channels):
            row = tails[k, pl.ds(place[0] * channels + c, 1), :]
            closing[pl.ds(c, 1), pl.ds(k * LANES, LANES)] = row
    row = row_of((channels, LANES))
    moves = jnp.zeros((channels, LANES), jnp.int32)
    for c in range(channels):
        moves = jnp.where(row == c, lags[place[0] * channels + c], moves)
    lag[...] = moves


def stage(channels, record_tail, lag_shift, place):
    vmem = pl.BlockSpec(memory_space=pltpu.VMEM)
    smem = pl.BlockSpec(memory_space=pltpu.SMEM)
    return pl.pallas_call(
        functools.partial(stage_kernel, channels),
        out_shape=(
            jax.ShapeDtypeStruct((channels, 2 * LANES), jnp.float32),
            jax.ShapeDtypeStruct((channels, LANES), jnp.int32),
        ),
        in_specs=[smem, smem, vmem],
        out_specs=(vmem, vmem),
        scratch_shapes=[
            pltpu.VMEM((2 * LANES, LANES), jnp.float32),
            pltpu.VMEM((2, LANES, LANES), jnp.float32),
        ],
        compiler_params=pltpu.CompilerParams(vmem_limit_bytes=4 * 1024 * 1024),
        cost_estimate=pl.CostEstimate(flops=3 * 10**9, bytes_accessed=10**6, transcendentals=0),
        name="stage",
    )(place, lag_shift, record_tail)


def align_kernel(channels, place, records, following, closing, lag, out, rows):
    rows[...] = jnp.zeros_like(rows)
    last = place[1] == 1
    own = records[...].astype(jnp.float32)
    after = following[:, : 2 * LANES].astype(jnp.float32)
    after = jnp.where(last, closing[...], after)
    x = [own[:, LANES * k : LANES * (k + 1)] for k in range(BLOCKS)]
    x += [after[:, :LANES], after[:, LANES:]]
    lane = lane_of((channels, LANES))
    for bit in range(5):
        step = 1 << bit
        rolled = [pltpu.roll(v, LANES - step, 1) for v in x]
        moved = (lag[...] & step) != 0
        inside = lane < LANES - step
        x = [
            jnp.where(moved, jnp.where(inside, rolled[k], rolled[min(k + 1, SPANS)]), x[k])
            for k in range(SPANS + 1)
        ]
    for k in range(SPANS):
        rows[pl.ds(k * channels, channels), :] = mirrored(x[k])
    out[...] = rows[...].astype(jnp.bfloat16)


def align(records, following, closing, lag, place):
    channels = records.shape[0]
    held = -(-SPANS * channels // 16) * 16
    vmem = pl.BlockSpec(memory_space=pltpu.VMEM)
    smem = pl.BlockSpec(memory_space=pltpu.SMEM)
    return pl.pallas_call(
        functools.partial(align_kernel, channels),
        out_shape=jax.ShapeDtypeStruct((held, LANES), jnp.bfloat16),
        in_specs=[smem, vmem, vmem, vmem, vmem],
        out_specs=vmem,
        scratch_shapes=[pltpu.VMEM((held, LANES), jnp.float32)],
        compiler_params=pltpu.CompilerParams(vmem_limit_bytes=4 * 1024 * 1024),
        cost_estimate=pl.CostEstimate(flops=3 * 10**9, bytes_accessed=10**6, transcendentals=0),
        name="align",
    )(place, records, following, closing, lag)


def over_rows(values):
    while len(values) > 1:
        values = [
            values[k] + values[k + 1] if k + 1 < len(values) else values[k]
            for k in range(0, len(values), 2)
        ]
    return jnp.sum(values[0], axis=0, keepdims=True)


def panel_kernel(begin, steps, place, templates, mask, out, weight, chosen, scaled):
    count = templates.shape[1]

    @pl.when(pl.program_id(0) == 0)
    def _():
        half = mask.shape[0] // 2
        used = mask[...].astype(jnp.float32)
        chosen[...] = jnp.where(place[1] == 1, used[half:], used[:half])
        scale = jnp.sqrt(L / jnp.sum(used, axis=0, keepdims=True))
        weight[...] = jnp.broadcast_to(scale, (LANES, count)).T
        scaled[pl.ds(ROWS, DEPTH - ROWS), :] = jnp.zeros((DEPTH - ROWS, count), scaled.dtype)

    row = row_of((8, count))
    middle = L // 8
    tiles = 2 * middle + 1
    first = ((begin + pl.program_id(0)) ^ (place[0] % steps)) * STEP

    def read(pair, t):
        at = pair * 2 * L + 8 * t
        held = templates[pl.ds(at // 16 * 16, 16), :].astype(jnp.float32)
        return held[at % 16 : at % 16 + 8]

    def both(pair, value):
        shared = value(middle)
        early = over_rows([value(t) for t in range(middle)] + [jnp.where(row < 4, shared, 0.0)])
        late = over_rows(
            [jnp.where(row < 4, 0.0, shared)] + [value(t) for t in range(middle + 1, tiles)]
        )
        return early, late

    def pick(values, pair, t):
        a, b = values[2 * pair], values[2 * pair + 1]
        if t == middle:
            return jnp.where(row < 4, a, b)
        return a if t < middle else b

    mean = []
    for pair in range(STEP // 2):
        mean += [v * (1.0 / L) for v in both(pair, lambda t: read(pair, t))]
    scale = []
    for pair in range(STEP // 2):

        def squared(t):
            u = read(pair, t) - pick(mean, pair, t)
            scaled[pl.ds(pair * 2 * L + 8 * t, 8), :] = u
            return u * u

        energies = both(pair, squared)
        for c in range(2):
            used = chosen[pl.ds(first + 2 * pair + c, 1), :]
            scale.append(lax.rsqrt(energies[c] + EPSILON) * used)
    for pair in range(STEP // 2):
        for t in range(tiles):
            at = pl.ds(pair * 2 * L + 8 * t, 8)
            scaled[at, :] = scaled[at, :] * pick(scale, pair, t)
    for k in range(DEPTH // LANES):
        part = scaled[pl.ds(LANES * k, LANES), :].astype(jnp.bfloat16)
        out[0, :, pl.ds(LANES * k, LANES)] = part.T


def normalized(templates, channel_mask, place, begin, steps):
    width, rows = templates.shape
    every = width // ROWS
    return pl.pallas_call(
        functools.partial(panel_kernel, begin, every),
        out_shape=(
            jax.ShapeDtypeStruct((steps, rows, DEPTH), jnp.bfloat16),
            jax.ShapeDtypeStruct((rows, LANES), jnp.float32),
        ),
        grid_spec=pltpu.PrefetchScalarGridSpec(
            num_scalar_prefetch=1,
            grid=(steps,),
            in_specs=[
                pl.BlockSpec((ROWS, rows), lambda i, at: ((i + begin) ^ (at[0] % every), 0)),
                pl.BlockSpec(memory_space=pltpu.VMEM),
            ],
            out_specs=(
                pl.BlockSpec((1, rows, DEPTH), lambda i, at: (i, 0, 0)),
                pl.BlockSpec((rows, LANES), lambda i, at: (0, 0)),
            ),
            scratch_shapes=[
                pltpu.VMEM((channel_mask.shape[0] // 2, rows), jnp.float32),
                pltpu.VMEM((DEPTH, rows), jnp.float32),
            ],
        ),
        compiler_params=pltpu.CompilerParams(vmem_limit_bytes=24 * 1024 * 1024),
        cost_estimate=pl.CostEstimate(
            flops=2 * 10**9, bytes_accessed=3 * 10**6, transcendentals=0
        ),
        name="panel",
    )(place, templates, channel_mask)


def prepare(samples, staged, left, spread, groups):
    at = natural(row_of((3 * LANES, 2 * LANES)))
    to = natural(lane_of((3 * LANES, 2 * LANES)))
    band = (at >= to) & (at < to + L)
    band = jnp.where(band, 1.0, 0.0).astype(jnp.bfloat16)
    rows = 16 * groups
    for g in range(groups):
        staged[g] = samples[g].astype(jnp.float32)
    for g in range(groups):
        for k in range(SPANS):
            x = staged[g, pl.ds(min(STEP * k, SPANS * STEP + 4 - 16), 16), :]
            cut = pl.ds(LANES * k, LANES)
            square = x * x
            high = square.astype(jnp.bfloat16)
            left[pl.ds(16 * g, 16), cut] = x.astype(jnp.bfloat16)
            left[pl.ds(rows + 16 * g, 16), cut] = high
            low = square - high.astype(jnp.float32)
            left[pl.ds(2 * rows + 16 * g, 16), cut] = low.astype(jnp.bfloat16)
    for q in range(BLOCKS // 2):
        cut = left[:, pl.ds(2 * LANES * q, 3 * LANES)]
        sums = jnp.dot(cut, band, preferred_element_type=jnp.float32)
        first = sums[:rows]
        second = sums[rows : 2 * rows] + sums[2 * rows :]
        scale = lax.rsqrt(second - first * first / L + L * EPSILON)
        spread[2 * q] = scale[:, :LANES]
        spread[2 * q + 1] = scale[:, LANES:]


def arrange(runs, scales, staged, spread, g):
    lane = lane_of((16, LANES))
    inverse = swap_runs([spread[b, pl.ds(16 * g, 16), :] for b in range(BLOCKS)])
    tail = staged[g, pl.ds(STEP * BLOCKS, 16), :]
    z = swap_runs([staged[g, pl.ds(STEP * k, 16), :] for k in range(BLOCKS)])
    for b in range(BLOCKS):
        scales[g, b] = inverse[b]
        runs[g, b] = z[b]
    for b in range(TILES + 1 - BLOCKS):
        turned = pltpu.roll(tail, LANES - RUN - RUN * b, 1)
        runs[g, BLOCKS + b] = jnp.where(
            lane < LANES - RUN, pltpu.roll(z[b], LANES - RUN, 1), turned
        )


def shifted_rows(runs, g, shifted):
    lane = lane_of((8, LANES)) & (RUN - 1)
    row = row_of((8, LANES))
    early = [pltpu.roll(runs[g, b], LANES - 4, 1) for b in range(TILES)]
    for c in range(STEP):
        offset = c * L % 16
        z = [
            jnp.broadcast_to(runs[g, b, pl.ds(c, 1), :], (8, LANES)) for b in range(TILES + 1)
        ]
        for b in range(TILES):
            halves = []
            for begin in (-offset, 8 - offset):
                move = row + begin
                if begin == -4:
                    here = sheared(jnp.broadcast_to(early[b][c : c + 1], (8, LANES)), 0)
                else:
                    here = sheared(z[b], begin)
                before = after = None
                if begin < 0:
                    before = jnp.where(lane < move + RUN, here, sheared(z[max(b - 1, 0)], begin + RUN))
                if begin + 7 >= 0:
                    after = jnp.where(lane >= move, here, sheared(z[b + 1], begin - RUN))
                if before is None:
                    halves.append(after)
                elif after is None:
                    halves.append(before)
                else:
                    halves.append(jnp.where(move < 0, before, after))
            shifted[c, pl.ds(16 * b, 16), :] = jnp.concatenate(halves, axis=0).astype(jnp.bfloat16)


def hankel_rows(shifted, scales, g, hankel):
    row = row_of((16, LANES))
    for b in range(BLOCKS):
        scale = [
            jnp.broadcast_to(scales[g, b, pl.ds(c, 1), :], (16, LANES)).astype(jnp.bfloat16)
            for c in range(STEP)
        ]

        def tile(c, q):
            return shifted[c, pl.ds(16 * (q - c * L // 16 + b), 16), :] * scale[c]

        for q in range(ROWS // 16):
            c = 16 * q // L
            value = tile(c, q)
            if c + 1 < STEP and 16 * q + 16 > (c + 1) * L:
                value = jnp.where(row < (c + 1) * L - 16 * q, value, tile(c + 1, q))
            hankel[pl.ds(16 * q, 16), pl.ds(LANES * b, LANES)] = value


def product_kernel(closing, parts, begin, half, order, samples, *rest):
    panels = rest[: 2 * parts]
    rest = rest[2 * parts :]
    if closing:
        weight, before, out = rest[:3]
        total, staging, sem = rest[-3:]
        rest = rest[3:-3]
    else:
        total = rest[0]
        rest = rest[1:]
    runs, scales, staged, left, spread, shifted, hankel_a, hankel_b = rest
    groups = samples.shape[0]
    prepare(samples, staged, left, spread, groups)
    hankels = (hankel_a, hankel_b)
    for hankel in hankels:
        hankel[pl.ds(ROWS, DEPTH - ROWS), :] = jnp.zeros(
            (DEPTH - ROWS, hankel.shape[1]), jnp.bfloat16
        )

    def fill(g, hankel):
        arrange(runs, scales, staged, spread, g)
        shifted_rows(runs, g, shifted)
        hankel_rows(shifted, scales, g, hankel)

    own = ((begin ^ order[0]) // half) == order[1]

    def panel(g):
        each = half // parts
        return jnp.where(own, panels[g // each][g % each], panels[parts + g // each][g % each])

    copies = []

    def finish(begin, size):
        for r in range(begin, begin + size, 8):
            cut = pl.ds(r, 8)
            blocks = [total[cut, LANES * b : LANES * (b + 1)] for b in range(BLOCKS)]
            blocks = swap_runs(blocks, mirror=True)
            for b in range(BLOCKS):
                staging[cut, LANES * b : LANES * (b + 1)] = blocks[b] * weight[cut, :]
            if (r + 8) % 32 == 0:
                rows = pl.ds(r - 24, 32)
                copies.append(
                    pltpu.make_async_copy(staging.at[rows], out.at[rows], sem.at[len(copies)])
                )
                copies[-1].start()

    fill(0, hankel_a)
    for g in range(groups):
        if g + 1 < groups:
            fill(g + 1, hankels[(g + 1) % 2])
        held = panel(g)
        final = closing and g == groups - 1
        size = min(128, held.shape[0]) if final else held.shape[0]
        for r in range(0, held.shape[0], size):
            rows = pl.ds(r, size)
            for q in range(BLOCKS // 2):
                cut = pl.ds(2 * LANES * q, 2 * LANES)
                value = jnp.dot(
                    held[r : r + size], hankels[g % 2][:, cut], preferred_element_type=jnp.float32
                )
                if g:
                    total[rows, cut] += value
                elif closing:
                    total[rows, cut] = before[rows, cut] + value
                else:
                    total[rows, cut] = value
            if final:
                finish(r, size)
    if closing:
        for copy in copies:
            copy.wait()


def product(order, samples, panels, begin, closing=None):
    groups = samples.shape[0]
    height = panels[0].shape[1]
    half = sum(panel.shape[0] for panel in panels) // 2
    vmem = pl.BlockSpec(memory_space=pltpu.VMEM)
    held = SPANS * STEP + 4
    extra = () if closing is None else closing
    scratch = [
        pltpu.VMEM((groups, TILES + 1, 16, LANES), jnp.float32),
        pltpu.VMEM((groups, BLOCKS, 16, LANES), jnp.float32),
        pltpu.VMEM((groups, held, LANES), jnp.float32),
        pltpu.VMEM((3 * 16 * groups, SPANS * LANES), jnp.bfloat16),
        pltpu.VMEM((BLOCKS, 16 * groups, LANES), jnp.float32),
        pltpu.VMEM((STEP, TILES * 16, LANES), jnp.bfloat16),
        pltpu.VMEM((DEPTH, BLOCKS * LANES), jnp.bfloat16),
        pltpu.VMEM((DEPTH, BLOCKS * LANES), jnp.bfloat16),
    ]
    if closing is not None:
        scratch += [
            pltpu.VMEM((height, BLOCKS * LANES), jnp.float32),
            pltpu.VMEM((height, BLOCKS * LANES), jnp.float32),
            pltpu.SemaphoreType.DMA((height // 32,)),
        ]
    return pl.pallas_call(
        functools.partial(
            product_kernel, closing is not None, len(panels) // 2, begin, half
        ),
        out_shape=jax.ShapeDtypeStruct((height, BLOCKS * LANES), jnp.float32),
        in_specs=[pl.BlockSpec(memory_space=pltpu.SMEM)] + [vmem] * (1 + len(panels) + len(extra)),
        out_specs=vmem if closing is None else pl.BlockSpec(memory_space=pl.ANY),
        scratch_shapes=scratch,
        compiler_params=pltpu.CompilerParams(vmem_limit_bytes=20 * 1024 * 1024),
        cost_estimate=pl.CostEstimate(
            flops=2 * height * groups * ROWS * BLOCKS * LANES,
            bytes_accessed=2 * groups * height * DEPTH + 4 * height * BLOCKS * LANES,
            transcendentals=0,
        ),
        name="product",
    )(order, samples, *panels, *extra)


def per_device(records, record_tail, templates, channel_mask, lag_shift):
    me = lax.axis_index("tmpl")
    devices = lax.axis_size("tmpl")
    core = lax.axis_index("tm")
    cores = lax.axis_size("tm")
    channels = records.shape[0]
    groups = lag_shift.shape[0] // STEP
    half = groups // cores
    place = jnp.stack([me, core]).astype(jnp.int32)
    templates = templates.T
    channel_mask = channel_mask.T
    pairs = [(0, 1), (1, 0)]
    following = lax.ppermute(records, "tm", [(i + 1, i) for i in range(cores - 1)])
    closing, lag = stage(channels, record_tail.T, lag_shift, place)
    aligned = align(records, following, closing, lag, place)
    doubling = channels == STEP and devices & (devices - 1) == 0
    ahead = (0, half // 2)
    parts = []
    held = received = aligned[None]
    reach = 1
    order = place if doubling else place * jnp.array([0, 1], jnp.int32)
    begun, received = lax.optimization_barrier((order, received))
    while reach < devices:
        if doubling:
            if reach > 1:
                held = jnp.concatenate([held, received], axis=0)
            received = lax.ppermute(held, "tmpl", [(i, i ^ reach) for i in range(devices)])
        if len(parts) < 2:
            part, weight = normalized(templates, channel_mask, begun, ahead[len(parts)], half // 2)
            part, received, begun = lax.optimization_barrier((part, received, begun))
            parts.append(part)
        reach *= 2
    panels = parts + [lax.ppermute(part, "tm", pairs) for part in parts]
    if doubling:
        near, far = held, received
    else:
        held = lax.all_gather(aligned, "tmpl", axis=0)
        held = held[:, : SPANS * channels].reshape(groups, STEP // channels, SPANS, channels, LANES)
        held = jnp.moveaxis(held, 1, 2).reshape(groups, SPANS * STEP, LANES)
        held = jnp.pad(held, ((0, 0), (0, 4), (0, 0)))
        near, far = held[:half], held[half:]
    total = product(order, near, panels, 0)
    return product(order, far, panels, half, (weight, total))


def solution(mesh):
    placed = (P("tmpl", ("win", "tm")), P(None, "win"), P("tmpl", "tm"), P("tmpl", None), P("win"))
    return jax.shard_map(
        per_device, mesh=mesh, in_specs=placed, out_specs=P("tmpl", ("win", "tm")), check_vma=False
    )
```

```python
import functools

import jax
import jax.numpy as jnp
from jax import lax
from jax.experimental import pallas as pl
from jax.experimental.pallas import tpu as pltpu
from jax.sharding import PartitionSpec as P

L = 100
LAGS = 32
EPSILON = 1e-05

LANES = 128
RUN = 16
STEP = 12
ROWS = STEP * L
DEPTH = 1280
BLOCKS = 8
SPANS = 9
TILES = 14
PARTS = 2


def lane_of(shape):
    return lax.broadcasted_iota(jnp.int32, shape, len(shape) - 1)


def row_of(shape):
    return lax.broadcasted_iota(jnp.int32, shape, 0)


def natural(index):
    return (index & ~(RUN - 1)) + (RUN - 1) - (index & (RUN - 1))


def mirrored(x):
    return jnp.take_along_axis(x, natural(lane_of(x.shape)), axis=1)


def turned_runs(x, by):
    by = by % BLOCKS
    return pltpu.roll(x, RUN * by, 1) if by else x


def swap_runs(blocks, mirror=False):
    lane = lane_of(blocks[0].shape)
    held = []
    for k in range(BLOCKS):
        by = -k % BLOCKS
        x = blocks[by]
        if mirror:
            source = natural((lane - RUN * by) & (LANES - 1))
            held.append(jnp.take_along_axis(x, source, axis=1))
        else:
            held.append(turned_runs(x, by))
    for bit in range(3):
        taken = (lane & (RUN << bit)) != 0
        held = [jnp.where(taken, held[(k - (1 << bit)) % BLOCKS], held[k]) for k in range(BLOCKS)]
    return [turned_runs(held[k], -k) for k in range(BLOCKS)]


def sheared(x, first):
    return pltpu.roll(x, first % LANES, 1, stride=1, stride_axis=0)


def stage_kernel(channels, place, lags, tail, closing, lag, turned, tails):
    turned[...] = jnp.zeros_like(turned)
    width, count = tail.shape
    turned[pl.ds(0, width), pl.ds(0, count)] = tail[...].astype(jnp.float32)
    for k in range(2):
        tails[k] = turned[pl.ds(LANES * k, LANES), :].T
    for k in range(2):
        for c in range(channels):
            row = tails[k, pl.ds(place[0] * channels + c, 1), :]
            closing[pl.ds(c, 1), pl.ds(k * LANES, LANES)] = row
    row = row_of((channels, LANES))
    moves = jnp.zeros((channels, LANES), jnp.int32)
    for c in range(channels):
        moves = jnp.where(row == c, lags[place[0] * channels + c], moves)
    lag[...] = moves


def stage(channels, record_tail, lag_shift, place):
    vmem = pl.BlockSpec(memory_space=pltpu.VMEM)
    smem = pl.BlockSpec(memory_space=pltpu.SMEM)
    return pl.pallas_call(
        functools.partial(stage_kernel, channels),
        out_shape=(
            jax.ShapeDtypeStruct((channels, 2 * LANES), jnp.float32),
            jax.ShapeDtypeStruct((channels, LANES), jnp.int32),
        ),
        in_specs=[smem, smem, vmem],
        out_specs=(vmem, vmem),
        scratch_shapes=[
            pltpu.VMEM((2 * LANES, LANES), jnp.float32),
            pltpu.VMEM((2, LANES, LANES), jnp.float32),
        ],
        compiler_params=pltpu.CompilerParams(vmem_limit_bytes=4 * 1024 * 1024),
        cost_estimate=pl.CostEstimate(flops=3 * 10**9, bytes_accessed=10**6, transcendentals=0),
        name="stage",
    )(place, lag_shift, record_tail)


def align_kernel(channels, place, records, following, closing, lag, out, rows):
    rows[...] = jnp.zeros_like(rows)
    last = place[1] == 1
    own = records[...].astype(jnp.float32)
    after = following[:, : 2 * LANES].astype(jnp.float32)
    after = jnp.where(last, closing[...], after)
    x = [own[:, LANES * k : LANES * (k + 1)] for k in range(BLOCKS)]
    x += [after[:, :LANES], after[:, LANES:]]
    lane = lane_of((channels, LANES))
    for bit in range(5):
        step = 1 << bit
        rolled = [pltpu.roll(v, LANES - step, 1) for v in x]
        moved = (lag[...] & step) != 0
        inside = lane < LANES - step
        x = [
            jnp.where(moved, jnp.where(inside, rolled[k], rolled[min(k + 1, SPANS)]), x[k])
            for k in range(SPANS + 1)
        ]
    for k in range(SPANS):
        rows[pl.ds(k * channels, channels), :] = mirrored(x[k])
    out[...] = rows[...].astype(jnp.bfloat16)


def align(records, following, closing, lag, place):
    channels = records.shape[0]
    held = -(-SPANS * channels // 16) * 16
    vmem = pl.BlockSpec(memory_space=pltpu.VMEM)
    smem = pl.BlockSpec(memory_space=pltpu.SMEM)
    return pl.pallas_call(
        functools.partial(align_kernel, channels),
        out_shape=jax.ShapeDtypeStruct((held, LANES), jnp.bfloat16),
        in_specs=[smem, vmem, vmem, vmem, vmem],
        out_specs=vmem,
        scratch_shapes=[pltpu.VMEM((held, LANES), jnp.float32)],
        compiler_params=pltpu.CompilerParams(vmem_limit_bytes=4 * 1024 * 1024),
        cost_estimate=pl.CostEstimate(flops=3 * 10**9, bytes_accessed=10**6, transcendentals=0),
        name="align",
    )(place, records, following, closing, lag)


def over_rows(values):
    while len(values) > 1:
        values = [
            values[k] + values[k + 1] if k + 1 < len(values) else values[k]
            for k in range(0, len(values), 2)
        ]
    return jnp.sum(values[0], axis=0, keepdims=True)


def panel_kernel(begin, steps, place, templates, mask, out, weight, chosen, scaled):
    count = templates.shape[1]

    @pl.when(pl.program_id(0) == 0)
    def _():
        half = mask.shape[0] // 2
        used = mask[...].astype(jnp.float32)
        chosen[...] = jnp.where(place[1] == 1, used[half:], used[:half])
        scale = jnp.sqrt(L / jnp.sum(used, axis=0, keepdims=True))
        weight[...] = jnp.broadcast_to(scale, (LANES, count)).T
        scaled[pl.ds(ROWS, DEPTH - ROWS), :] = jnp.zeros((DEPTH - ROWS, count), scaled.dtype)

    row = row_of((8, count))
    middle = L // 8
    tiles = 2 * middle + 1
    first = ((PARTS * pl.program_id(0) + begin) ^ (place[0] % steps)) * STEP

    def read(pair, t):
        at = pair * 2 * L + 8 * t
        held = templates[pl.ds(at // 16 * 16, 16), :].astype(jnp.float32)
        return held[at % 16 : at % 16 + 8]

    def both(pair, value):
        shared = value(middle)
        early = over_rows([value(t) for t in range(middle)] + [jnp.where(row < 4, shared, 0.0)])
        late = over_rows(
            [jnp.where(row < 4, 0.0, shared)] + [value(t) for t in range(middle + 1, tiles)]
        )
        return early, late

    def pick(values, pair, t):
        a, b = values[2 * pair], values[2 * pair + 1]
        if t == middle:
            return jnp.where(row < 4, a, b)
        return a if t < middle else b

    mean = []
    for pair in range(STEP // 2):
        mean += [v * (1.0 / L) for v in both(pair, lambda t: read(pair, t))]
    scale = []
    for pair in range(STEP // 2):

        def squared(t):
            u = read(pair, t) - pick(mean, pair, t)
            scaled[pl.ds(pair * 2 * L + 8 * t, 8), :] = u
            return u * u

        energies = both(pair, squared)
        for c in range(2):
            used = chosen[pl.ds(first + 2 * pair + c, 1), :]
            scale.append(lax.rsqrt(energies[c] + EPSILON) * used)
    for pair in range(STEP // 2):
        for t in range(tiles):
            at = pl.ds(pair * 2 * L + 8 * t, 8)
            scaled[at, :] = scaled[at, :] * pick(scale, pair, t)
    for k in range(DEPTH // LANES):
        part = scaled[pl.ds(LANES * k, LANES), :].astype(jnp.bfloat16)
        out[0, :, pl.ds(LANES * k, LANES)] = part.T


def normalized(templates, channel_mask, place, begin, steps):
    width, rows = templates.shape
    every = width // ROWS
    return pl.pallas_call(
        functools.partial(panel_kernel, begin, every),
        out_shape=(
            jax.ShapeDtypeStruct((steps, rows, DEPTH), jnp.bfloat16),
            jax.ShapeDtypeStruct((rows, LANES), jnp.float32),
        ),
        grid_spec=pltpu.PrefetchScalarGridSpec(
            num_scalar_prefetch=1,
            grid=(steps,),
            in_specs=[
                pl.BlockSpec((ROWS, rows), lambda i, at: ((PARTS * i + begin) ^ (at[0] % every), 0)),
                pl.BlockSpec(memory_space=pltpu.VMEM),
            ],
            out_specs=(
                pl.BlockSpec((1, rows, DEPTH), lambda i, at: (i, 0, 0)),
                pl.BlockSpec((rows, LANES), lambda i, at: (0, 0)),
            ),
            scratch_shapes=[
                pltpu.VMEM((channel_mask.shape[0] // 2, rows), jnp.float32),
                pltpu.VMEM((DEPTH, rows), jnp.float32),
            ],
        ),
        compiler_params=pltpu.CompilerParams(vmem_limit_bytes=24 * 1024 * 1024),
        cost_estimate=pl.CostEstimate(
            flops=2 * 10**9, bytes_accessed=3 * 10**6, transcendentals=0
        ),
        name="panel",
    )(place, templates, channel_mask)


def prepare(samples, staged, left, spread, groups):
    at = natural(row_of((3 * LANES, 2 * LANES)))
    to = natural(lane_of((3 * LANES, 2 * LANES)))
    band = (at >= to) & (at < to + L)
    band = jnp.where(band, 1.0, 0.0).astype(jnp.bfloat16)
    rows = 16 * groups
    for g in range(groups):
        staged[g] = samples[g].astype(jnp.float32)
    for g in range(groups):
        for k in range(SPANS):
            x = staged[g, pl.ds(min(STEP * k, SPANS * STEP + 4 - 16), 16), :]
            cut = pl.ds(LANES * k, LANES)
            square = x * x
            high = square.astype(jnp.bfloat16)
            left[pl.ds(16 * g, 16), cut] = x.astype(jnp.bfloat16)
            left[pl.ds(rows + 16 * g, 16), cut] = high
            low = square - high.astype(jnp.float32)
            left[pl.ds(2 * rows + 16 * g, 16), cut] = low.astype(jnp.bfloat16)
    for q in range(BLOCKS // 2):
        cut = left[:, pl.ds(2 * LANES * q, 3 * LANES)]
        sums = jnp.dot(cut, band, preferred_element_type=jnp.float32)
        first = sums[:rows]
        second = sums[rows : 2 * rows] + sums[2 * rows :]
        scale = lax.rsqrt(second - first * first / L + L * EPSILON)
        spread[2 * q] = scale[:, :LANES]
        spread[2 * q + 1] = scale[:, LANES:]


def arrange(runs, scales, staged, spread, g):
    lane = lane_of((16, LANES))
    inverse = swap_runs([spread[b, pl.ds(16 * g, 16), :] for b in range(BLOCKS)])
    tail = staged[g, pl.ds(STEP * BLOCKS, 16), :]
    z = swap_runs([staged[g, pl.ds(STEP * k, 16), :] for k in range(BLOCKS)])
    for b in range(BLOCKS):
        scales[g, b] = inverse[b]
        runs[g, b] = z[b]
    for b in range(TILES + 1 - BLOCKS):
        turned = pltpu.roll(tail, LANES - RUN - RUN * b, 1)
        runs[g, BLOCKS + b] = jnp.where(
            lane < LANES - RUN, pltpu.roll(z[b], LANES - RUN, 1), turned
        )


def shifted_rows(runs, g, shifted):
    lane = lane_of((8, LANES)) & (RUN - 1)
    row = row_of((8, LANES))
    early = [pltpu.roll(runs[g, b], LANES - 4, 1) for b in range(TILES)]
    for c in range(STEP):
        offset = c * L % 16
        z = [
            jnp.broadcast_to(runs[g, b, pl.ds(c, 1), :], (8, LANES)) for b in range(TILES + 1)
        ]
        for b in range(TILES):
            halves = []
            for begin in (-offset, 8 - offset):
                move = row + begin
                if begin == -4:
                    here = sheared(jnp.broadcast_to(early[b][c : c + 1], (8, LANES)), 0)
                else:
                    here = sheared(z[b], begin)
                before = after = None
                if begin < 0:
                    before = jnp.where(lane < move + RUN, here, sheared(z[max(b - 1, 0)], begin + RUN))
                if begin + 7 >= 0:
                    after = jnp.where(lane >= move, here, sheared(z[b + 1], begin - RUN))
                if before is None:
                    halves.append(after)
                elif after is None:
                    halves.append(before)
                else:
                    halves.append(jnp.where(move < 0, before, after))
            shifted[c, pl.ds(16 * b, 16), :] = jnp.concatenate(halves, axis=0).astype(jnp.bfloat16)


def hankel_rows(shifted, scales, g, hankel):
    row = row_of((16, LANES))
    for b in range(BLOCKS):
        scale = [
            jnp.broadcast_to(scales[g, b, pl.ds(c, 1), :], (16, LANES)).astype(jnp.bfloat16)
            for c in range(STEP)
        ]

        def tile(c, q):
            return shifted[c, pl.ds(16 * (q - c * L // 16 + b), 16), :] * scale[c]

        for q in range(ROWS // 16):
            c = 16 * q // L
            value = tile(c, q)
            if c + 1 < STEP and 16 * q + 16 > (c + 1) * L:
                value = jnp.where(row < (c + 1) * L - 16 * q, value, tile(c + 1, q))
            hankel[pl.ds(16 * q, 16), pl.ds(LANES * b, LANES)] = value


def product_kernel(closing, slots, half, order, samples, *rest):
    mine, theirs = rest[:2]
    rest = rest[2:]
    if closing:
        weight, before, out = rest[:3]
        total, staging, sem = rest[-3:]
        rest = rest[3:-3]
    else:
        total = rest[0]
        rest = rest[1:]
    runs, scales, staged, left, spread, shifted, hankel_a, hankel_b = rest
    groups = samples.shape[0]
    prepare(samples, staged, left, spread, groups)
    hankels = (hankel_a, hankel_b)
    for hankel in hankels:
        hankel[pl.ds(ROWS, DEPTH - ROWS), :] = jnp.zeros(
            (DEPTH - ROWS, hankel.shape[1]), jnp.bfloat16
        )

    def fill(g, hankel):
        arrange(runs, scales, staged, spread, g)
        shifted_rows(runs, g, shifted)
        hankel_rows(shifted, scales, g, hankel)

    def panel(g):
        own = ((slots[g] ^ order[0]) // half) == order[1]
        at = slots[g] % half // PARTS
        return jnp.where(own, mine[at], theirs[at])

    copies = []

    def finish(begin, size):
        for r in range(begin, begin + size, 8):
            cut = pl.ds(r, 8)
            blocks = [total[cut, LANES * b : LANES * (b + 1)] for b in range(BLOCKS)]
            blocks = swap_runs(blocks, mirror=True)
            for b in range(BLOCKS):
                staging[cut, LANES * b : LANES * (b + 1)] = blocks[b] * weight[cut, :]
            if (r + 8) % 32 == 0:
                rows = pl.ds(r - 24, 32)
                copies.append(
                    pltpu.make_async_copy(staging.at[rows], out.at[rows], sem.at[len(copies)])
                )
                copies[-1].start()

    fill(0, hankel_a)
    for g in range(groups):
        if g + 1 < groups:
            fill(g + 1, hankels[(g + 1) % 2])
        held = panel(g)
        final = closing and g == groups - 1
        size = min(128, held.shape[0]) if final else held.shape[0]
        for r in range(0, held.shape[0], size):
            rows = pl.ds(r, size)
            for q in range(BLOCKS // 2):
                cut = pl.ds(2 * LANES * q, 2 * LANES)
                value = jnp.dot(
                    held[r : r + size], hankels[g % 2][:, cut], preferred_element_type=jnp.float32
                )
                if g:
                    total[rows, cut] += value
                elif closing:
                    total[rows, cut] = before[rows, cut] + value
                else:
                    total[rows, cut] = value
            if final:
                finish(r, size)
    if closing:
        for copy in copies:
            copy.wait()


def product(order, samples, panels, slots, closing=None):
    groups = samples.shape[0]
    height = panels[0].shape[1]
    half = PARTS * panels[0].shape[0]
    vmem = pl.BlockSpec(memory_space=pltpu.VMEM)
    held = SPANS * STEP + 4
    extra = () if closing is None else closing
    scratch = [
        pltpu.VMEM((groups, TILES + 1, 16, LANES), jnp.float32),
        pltpu.VMEM((groups, BLOCKS, 16, LANES), jnp.float32),
        pltpu.VMEM((groups, held, LANES), jnp.float32),
        pltpu.VMEM((3 * 16 * groups, SPANS * LANES), jnp.bfloat16),
        pltpu.VMEM((BLOCKS, 16 * groups, LANES), jnp.float32),
        pltpu.VMEM((STEP, TILES * 16, LANES), jnp.bfloat16),
        pltpu.VMEM((DEPTH, BLOCKS * LANES), jnp.bfloat16),
        pltpu.VMEM((DEPTH, BLOCKS * LANES), jnp.bfloat16),
    ]
    if closing is not None:
        scratch += [
            pltpu.VMEM((height, BLOCKS * LANES), jnp.float32),
            pltpu.VMEM((height, BLOCKS * LANES), jnp.float32),
            pltpu.SemaphoreType.DMA((height // 32,)),
        ]
    return pl.pallas_call(
        functools.partial(
            product_kernel, closing is not None, tuple(slots), half
        ),
        out_shape=jax.ShapeDtypeStruct((height, BLOCKS * LANES), jnp.float32),
        in_specs=[pl.BlockSpec(memory_space=pltpu.SMEM)] + [vmem] * (1 + len(panels) + len(extra)),
        out_specs=vmem if closing is None else pl.BlockSpec(memory_space=pl.ANY),
        scratch_shapes=scratch,
        compiler_params=pltpu.CompilerParams(vmem_limit_bytes=20 * 1024 * 1024),
        cost_estimate=pl.CostEstimate(
            flops=2 * height * groups * ROWS * BLOCKS * LANES,
            bytes_accessed=2 * groups * height * DEPTH + 4 * height * BLOCKS * LANES,
            transcendentals=0,
        ),
        name="product",
    )(order, samples, *panels, *extra)


def per_device(records, record_tail, templates, channel_mask, lag_shift):
    me = lax.axis_index("tmpl")
    devices = lax.axis_size("tmpl")
    core = lax.axis_index("tm")
    cores = lax.axis_size("tm")
    channels = records.shape[0]
    groups = lag_shift.shape[0] // STEP
    half = groups // cores
    place = jnp.stack([me, core]).astype(jnp.int32)
    templates = templates.T
    channel_mask = channel_mask.T
    pairs = [(0, 1), (1, 0)]
    following = lax.ppermute(records, "tm", [(i + 1, i) for i in range(cores - 1)])
    closing, lag = stage(channels, record_tail.T, lag_shift, place)
    aligned = align(records, following, closing, lag, place)
    doubling = channels == STEP and devices == groups and devices & (devices - 1) == 0
    parts = []
    held = received = aligned[None]
    slots = [0]
    order = place if doubling else place * jnp.array([0, 1], jnp.int32)
    begun, received = lax.optimization_barrier((order, received))
    reach = groups // 2
    while reach:
        if doubling:
            if len(slots) > 1:
                held = jnp.concatenate([held, received], axis=0)
            received = lax.ppermute(held, "tmpl", [(i, i ^ reach) for i in range(devices)])
        if len(parts) < PARTS:
            part, weight = normalized(templates, channel_mask, begun, len(parts), half // PARTS)
            part, received, begun = lax.optimization_barrier((part, received, begun))
            parts.append(part)
        slots += [slot ^ reach for slot in slots]
        reach //= 2
    early, late = [(part, lax.ppermute(part, "tm", pairs)) for part in parts]
    if doubling:
        near, far = held, received
    else:
        held = lax.all_gather(aligned, "tmpl", axis=0)
        held = held[:, : SPANS * channels].reshape(groups, STEP // channels, SPANS, channels, LANES)
        held = jnp.moveaxis(held, 1, 2).reshape(groups, SPANS * STEP, LANES)
        held = jnp.pad(held, ((0, 0), (0, 4), (0, 0)))
        held = jnp.stack([held[slot] for slot in slots])
        near, far = held[:half], held[half:]
    total = product(order, near, early, slots[:half])
    return product(order, far, late, slots[half:], (weight, total))


def solution(mesh):
    placed = (P("tmpl", ("win", "tm")), P(None, "win"), P("tmpl", "tm"), P("tmpl", None), P("win"))
    return jax.shard_map(
        per_device, mesh=mesh, in_specs=placed, out_specs=P("tmpl", ("win", "tm")), check_vma=False
    )
```

```python
import functools

import jax
import jax.numpy as jnp
from jax import lax
from jax.experimental import pallas as pl
from jax.experimental.pallas import tpu as pltpu
from jax.sharding import PartitionSpec as P

L = 100
LAGS = 32
EPSILON = 1e-05

LANES = 128
RUN = 16
STEP = 12
ROWS = STEP * L
DEPTH = 1280
BLOCKS = 8
SPANS = 9
TILES = 14
PARTS = 2


def lane_of(shape):
    return lax.broadcasted_iota(jnp.int32, shape, len(shape) - 1)


def row_of(shape):
    return lax.broadcasted_iota(jnp.int32, shape, 0)


def natural(index):
    return (index & ~(RUN - 1)) + (RUN - 1) - (index & (RUN - 1))


def mirrored(x):
    return jnp.take_along_axis(x, natural(lane_of(x.shape)), axis=1)


def turned_runs(x, by):
    by = by % BLOCKS
    return pltpu.roll(x, RUN * by, 1) if by else x


def swap_runs(blocks, mirror=False):
    lane = lane_of(blocks[0].shape)
    held = []
    for k in range(BLOCKS):
        by = -k % BLOCKS
        x = blocks[by]
        if mirror:
            source = natural((lane - RUN * by) & (LANES - 1))
            held.append(jnp.take_along_axis(x, source, axis=1))
        else:
            held.append(turned_runs(x, by))
    for bit in range(3):
        taken = (lane & (RUN << bit)) != 0
        held = [jnp.where(taken, held[(k - (1 << bit)) % BLOCKS], held[k]) for k in range(BLOCKS)]
    return [turned_runs(held[k], -k) for k in range(BLOCKS)]


def sheared(x, first):
    return pltpu.roll(x, first % LANES, 1, stride=1, stride_axis=0)


def stage_kernel(channels, place, lags, tail, closing, lag, turned, tails):
    turned[...] = jnp.zeros_like(turned)
    width, count = tail.shape
    turned[pl.ds(0, width), pl.ds(0, count)] = tail[...].astype(jnp.float32)
    for k in range(2):
        tails[k] = turned[pl.ds(LANES * k, LANES), :].T
    for k in range(2):
        for c in range(channels):
            row = tails[k, pl.ds(place[0] * channels + c, 1), :]
            closing[pl.ds(c, 1), pl.ds(k * LANES, LANES)] = row
    row = row_of((channels, LANES))
    moves = jnp.zeros((channels, LANES), jnp.int32)
    for c in range(channels):
        moves = jnp.where(row == c, lags[place[0] * channels + c], moves)
    lag[...] = moves


def stage(channels, record_tail, lag_shift, place):
    vmem = pl.BlockSpec(memory_space=pltpu.VMEM)
    smem = pl.BlockSpec(memory_space=pltpu.SMEM)
    return pl.pallas_call(
        functools.partial(stage_kernel, channels),
        out_shape=(
            jax.ShapeDtypeStruct((channels, 2 * LANES), jnp.float32),
            jax.ShapeDtypeStruct((channels, LANES), jnp.int32),
        ),
        in_specs=[smem, smem, vmem],
        out_specs=(vmem, vmem),
        scratch_shapes=[
            pltpu.VMEM((2 * LANES, LANES), jnp.float32),
            pltpu.VMEM((2, LANES, LANES), jnp.float32),
        ],
        compiler_params=pltpu.CompilerParams(vmem_limit_bytes=4 * 1024 * 1024),
        cost_estimate=pl.CostEstimate(flops=3 * 10**9, bytes_accessed=10**6, transcendentals=0),
        name="stage",
    )(place, lag_shift, record_tail)


def align_kernel(channels, place, records, following, closing, lag, out, rows):
    rows[...] = jnp.zeros_like(rows)
    last = place[1] == 1
    own = records[...].astype(jnp.float32)
    after = following[:, : 2 * LANES].astype(jnp.float32)
    after = jnp.where(last, closing[...], after)
    x = [own[:, LANES * k : LANES * (k + 1)] for k in range(BLOCKS)]
    x += [after[:, :LANES], after[:, LANES:]]
    lane = lane_of((channels, LANES))
    for bit in range(5):
        step = 1 << bit
        rolled = [pltpu.roll(v, LANES - step, 1) for v in x]
        moved = (lag[...] & step) != 0
        inside = lane < LANES - step
        x = [
            jnp.where(moved, jnp.where(inside, rolled[k], rolled[min(k + 1, SPANS)]), x[k])
            for k in range(SPANS + 1)
        ]
    for k in range(SPANS):
        rows[pl.ds(k * channels, channels), :] = mirrored(x[k])
    out[...] = rows[...].astype(jnp.bfloat16)


def align(records, following, closing, lag, place):
    channels = records.shape[0]
    held = -(-SPANS * channels // 16) * 16
    vmem = pl.BlockSpec(memory_space=pltpu.VMEM)
    smem = pl.BlockSpec(memory_space=pltpu.SMEM)
    return pl.pallas_call(
        functools.partial(align_kernel, channels),
        out_shape=jax.ShapeDtypeStruct((held, LANES), jnp.bfloat16),
        in_specs=[smem, vmem, vmem, vmem, vmem],
        out_specs=vmem,
        scratch_shapes=[pltpu.VMEM((held, LANES), jnp.float32)],
        compiler_params=pltpu.CompilerParams(vmem_limit_bytes=4 * 1024 * 1024),
        cost_estimate=pl.CostEstimate(flops=3 * 10**9, bytes_accessed=10**6, transcendentals=0),
        name="align",
    )(place, records, following, closing, lag)


def over_rows(values):
    while len(values) > 1:
        values = [
            values[k] + values[k + 1] if k + 1 < len(values) else values[k]
            for k in range(0, len(values), 2)
        ]
    return jnp.sum(values[0], axis=0, keepdims=True)


def panel_kernel(begin, steps, place, templates, mask, out, weight, chosen, scaled):
    count = templates.shape[1]

    @pl.when(pl.program_id(0) == 0)
    def _():
        half = mask.shape[0] // 2
        used = mask[...].astype(jnp.float32)
        chosen[...] = jnp.where(place[1] == 1, used[half:], used[:half])
        scale = jnp.sqrt(L / jnp.sum(used, axis=0, keepdims=True))
        weight[...] = jnp.broadcast_to(scale, (LANES, count)).T
        scaled[pl.ds(ROWS, DEPTH - ROWS), :] = jnp.zeros((DEPTH - ROWS, count), scaled.dtype)

    row = row_of((8, count))
    middle = L // 8
    tiles = 2 * middle + 1
    first = ((PARTS * pl.program_id(0) + begin) ^ (place[0] % steps)) * STEP

    def read(pair, t):
        at = pair * 2 * L + 8 * t
        held = templates[pl.ds(at // 16 * 16, 16), :].astype(jnp.float32)
        return held[at % 16 : at % 16 + 8]

    def both(pair, value):
        shared = value(middle)
        early = over_rows([value(t) for t in range(middle)] + [jnp.where(row < 4, shared, 0.0)])
        late = over_rows(
            [jnp.where(row < 4, 0.0, shared)] + [value(t) for t in range(middle + 1, tiles)]
        )
        return early, late

    def pick(values, pair, t):
        a, b = values[2 * pair], values[2 * pair + 1]
        if t == middle:
            return jnp.where(row < 4, a, b)
        return a if t < middle else b

    mean = []
    for pair in range(STEP // 2):
        mean += [v * (1.0 / L) for v in both(pair, lambda t: read(pair, t))]
    scale = []
    for pair in range(STEP // 2):

        def squared(t):
            u = read(pair, t) - pick(mean, pair, t)
            scaled[pl.ds(pair * 2 * L + 8 * t, 8), :] = u
            return u * u

        energies = both(pair, squared)
        for c in range(2):
            used = chosen[pl.ds(first + 2 * pair + c, 1), :]
            scale.append(lax.rsqrt(energies[c] + EPSILON) * used)
    for pair in range(STEP // 2):
        for t in range(tiles):
            at = pl.ds(pair * 2 * L + 8 * t, 8)
            scaled[at, :] = scaled[at, :] * pick(scale, pair, t)
    for k in range(DEPTH // LANES):
        part = scaled[pl.ds(LANES * k, LANES), :].astype(jnp.bfloat16)
        out[0, :, pl.ds(LANES * k, LANES)] = part.T


def normalized(templates, channel_mask, place, begin, steps):
    width, rows = templates.shape
    every = width // ROWS
    return pl.pallas_call(
        functools.partial(panel_kernel, begin, every),
        out_shape=(
            jax.ShapeDtypeStruct((steps, rows, DEPTH), jnp.bfloat16),
            jax.ShapeDtypeStruct((rows, LANES), jnp.float32),
        ),
        grid_spec=pltpu.PrefetchScalarGridSpec(
            num_scalar_prefetch=1,
            grid=(steps,),
            in_specs=[
                pl.BlockSpec((ROWS, rows), lambda i, at: ((PARTS * i + begin) ^ (at[0] % every), 0)),
                pl.BlockSpec(memory_space=pltpu.VMEM),
            ],
            out_specs=(
                pl.BlockSpec((1, rows, DEPTH), lambda i, at: (i, 0, 0)),
                pl.BlockSpec((rows, LANES), lambda i, at: (0, 0)),
            ),
            scratch_shapes=[
                pltpu.VMEM((channel_mask.shape[0] // 2, rows), jnp.float32),
                pltpu.VMEM((DEPTH, rows), jnp.float32),
            ],
        ),
        compiler_params=pltpu.CompilerParams(vmem_limit_bytes=24 * 1024 * 1024),
        cost_estimate=pl.CostEstimate(
            flops=2 * 10**9, bytes_accessed=3 * 10**6, transcendentals=0
        ),
        name="panel",
    )(place, templates, channel_mask)


def prepare(samples, staged, left, spread, groups):
    at = natural(row_of((3 * LANES, 2 * LANES)))
    to = natural(lane_of((3 * LANES, 2 * LANES)))
    band = (at >= to) & (at < to + L)
    band = jnp.where(band, 1.0, 0.0).astype(jnp.bfloat16)
    rows = 16 * groups
    for g in range(groups):
        staged[g] = samples[g].astype(jnp.float32)
    for g in range(groups):
        for k in range(SPANS):
            x = staged[g, pl.ds(min(STEP * k, SPANS * STEP + 4 - 16), 16), :]
            cut = pl.ds(LANES * k, LANES)
            square = x * x
            high = square.astype(jnp.bfloat16)
            left[pl.ds(16 * g, 16), cut] = x.astype(jnp.bfloat16)
            left[pl.ds(rows + 16 * g, 16), cut] = high
            low = square - high.astype(jnp.float32)
            left[pl.ds(2 * rows + 16 * g, 16), cut] = low.astype(jnp.bfloat16)
    for q in range(BLOCKS // 2):
        cut = left[:, pl.ds(2 * LANES * q, 3 * LANES)]
        sums = jnp.dot(cut, band, preferred_element_type=jnp.float32)
        first = sums[:rows]
        second = sums[rows : 2 * rows] + sums[2 * rows :]
        scale = lax.rsqrt(second - first * first / L + L * EPSILON)
        spread[2 * q] = scale[:, :LANES]
        spread[2 * q + 1] = scale[:, LANES:]


def arrange(runs, scales, staged, spread, g):
    lane = lane_of((16, LANES))
    inverse = swap_runs([spread[b, pl.ds(16 * g, 16), :] for b in range(BLOCKS)])
    tail = staged[g, pl.ds(STEP * BLOCKS, 16), :]
    z = swap_runs([staged[g, pl.ds(STEP * k, 16), :] for k in range(BLOCKS)])
    for b in range(BLOCKS):
        scales[g, b] = inverse[b]
        runs[g, b] = z[b]
    for b in range(TILES + 1 - BLOCKS):
        turned = pltpu.roll(tail, LANES - RUN - RUN * b, 1)
        runs[g, BLOCKS + b] = jnp.where(
            lane < LANES - RUN, pltpu.roll(z[b], LANES - RUN, 1), turned
        )


def shifted_rows(runs, g, shifted):
    lane = lane_of((8, LANES)) & (RUN - 1)
    row = row_of((8, LANES))
    early = [pltpu.roll(runs[g, b], LANES - 4, 1) for b in range(TILES)]
    for c in range(STEP):
        offset = c * L % 16
        z = [
            jnp.broadcast_to(runs[g, b, pl.ds(c, 1), :], (8, LANES)) for b in range(TILES + 1)
        ]
        for b in range(TILES):
            halves = []
            for begin in (-offset, 8 - offset):
                move = row + begin
                if begin == -4:
                    here = sheared(jnp.broadcast_to(early[b][c : c + 1], (8, LANES)), 0)
                else:
                    here = sheared(z[b], begin)
                before = after = None
                if begin < 0:
                    before = jnp.where(lane < move + RUN, here, sheared(z[max(b - 1, 0)], begin + RUN))
                if begin + 7 >= 0:
                    after = jnp.where(lane >= move, here, sheared(z[b + 1], begin - RUN))
                if before is None:
                    halves.append(after)
                elif after is None:
                    halves.append(before)
                else:
                    halves.append(jnp.where(move < 0, before, after))
            shifted[c, pl.ds(16 * b, 16), :] = jnp.concatenate(halves, axis=0).astype(jnp.bfloat16)


def hankel_rows(shifted, scales, g, hankel):
    row = row_of((16, LANES))
    for b in range(BLOCKS):
        scale = [
            jnp.broadcast_to(scales[g, b, pl.ds(c, 1), :], (16, LANES)).astype(jnp.bfloat16)
            for c in range(STEP)
        ]

        def tile(c, q):
            return shifted[c, pl.ds(16 * (q - c * L // 16 + b), 16), :] * scale[c]

        for q in range(ROWS // 16):
            c = 16 * q // L
            value = tile(c, q)
            if c + 1 < STEP and 16 * q + 16 > (c + 1) * L:
                value = jnp.where(row < (c + 1) * L - 16 * q, value, tile(c + 1, q))
            hankel[pl.ds(16 * q, 16), pl.ds(LANES * b, LANES)] = value


def product_kernel(closing, slots, half, order, samples, *rest):
    mine, theirs = rest[:2]
    rest = rest[2:]
    if closing:
        weight, before, out = rest[:3]
        total, staging, sem = rest[-3:]
        rest = rest[3:-3]
    else:
        total = rest[0]
        rest = rest[1:]
    runs, scales, staged, left, spread, shifted, hankel_a, hankel_b = rest
    groups = samples.shape[0]
    prepare(samples, staged, left, spread, groups)
    hankels = (hankel_a, hankel_b)
    for hankel in hankels:
        hankel[pl.ds(ROWS, DEPTH - ROWS), :] = jnp.zeros(
            (DEPTH - ROWS, hankel.shape[1]), jnp.bfloat16
        )

    def fill(g, hankel):
        arrange(runs, scales, staged, spread, g)
        shifted_rows(runs, g, shifted)
        hankel_rows(shifted, scales, g, hankel)

    def panel(g):
        own = ((slots[g] ^ order[0]) // half) == order[1]
        at = slots[g] % half // PARTS
        return jnp.where(own, mine[at], theirs[at])

    copies = []

    def finish(begin, size):
        for r in range(begin, begin + size, 8):
            cut = pl.ds(r, 8)
            blocks = [total[cut, LANES * b : LANES * (b + 1)] for b in range(BLOCKS)]
            blocks = swap_runs(blocks, mirror=True)
            for b in range(BLOCKS):
                staging[cut, LANES * b : LANES * (b + 1)] = blocks[b] * weight[cut, :]
            if (r + 8) % 32 == 0:
                rows = pl.ds(r - 24, 32)
                copies.append(
                    pltpu.make_async_copy(staging.at[rows], out.at[rows], sem.at[len(copies)])
                )
                copies[-1].start()

    fill(0, hankel_a)
    for g in range(groups):
        if g + 1 < groups:
            fill(g + 1, hankels[(g + 1) % 2])
        held = panel(g)
        final = closing and g == groups - 1
        size = min(64, held.shape[0]) if final else held.shape[0]
        for r in range(0, held.shape[0], size):
            rows = pl.ds(r, size)
            for q in range(BLOCKS // 2):
                cut = pl.ds(2 * LANES * q, 2 * LANES)
                value = jnp.dot(
                    held[r : r + size], hankels[g % 2][:, cut], preferred_element_type=jnp.float32
                )
                if g:
                    total[rows, cut] += value
                elif closing:
                    total[rows, cut] = before[rows, cut] + value
                else:
                    total[rows, cut] = value
            if final:
                finish(r, size)
    if closing:
        for copy in copies:
            copy.wait()


def product(order, samples, panels, slots, closing=None):
    groups = samples.shape[0]
    height = panels[0].shape[1]
    half = PARTS * panels[0].shape[0]
    vmem = pl.BlockSpec(memory_space=pltpu.VMEM)
    held = SPANS * STEP + 4
    extra = () if closing is None else closing
    scratch = [
        pltpu.VMEM((groups, TILES + 1, 16, LANES), jnp.float32),
        pltpu.VMEM((groups, BLOCKS, 16, LANES), jnp.float32),
        pltpu.VMEM((groups, held, LANES), jnp.float32),
        pltpu.VMEM((3 * 16 * groups, SPANS * LANES), jnp.bfloat16),
        pltpu.VMEM((BLOCKS, 16 * groups, LANES), jnp.float32),
        pltpu.VMEM((STEP, TILES * 16, LANES), jnp.bfloat16),
        pltpu.VMEM((DEPTH, BLOCKS * LANES), jnp.bfloat16),
        pltpu.VMEM((DEPTH, BLOCKS * LANES), jnp.bfloat16),
    ]
    if closing is not None:
        scratch += [
            pltpu.VMEM((height, BLOCKS * LANES), jnp.float32),
            pltpu.VMEM((height, BLOCKS * LANES), jnp.float32),
            pltpu.SemaphoreType.DMA((height // 32,)),
        ]
    return pl.pallas_call(
        functools.partial(
            product_kernel, closing is not None, tuple(slots), half
        ),
        out_shape=jax.ShapeDtypeStruct((height, BLOCKS * LANES), jnp.float32),
        in_specs=[pl.BlockSpec(memory_space=pltpu.SMEM)] + [vmem] * (1 + len(panels) + len(extra)),
        out_specs=vmem if closing is None else pl.BlockSpec(memory_space=pl.ANY),
        scratch_shapes=scratch,
        compiler_params=pltpu.CompilerParams(vmem_limit_bytes=20 * 1024 * 1024),
        cost_estimate=pl.CostEstimate(
            flops=2 * height * groups * ROWS * BLOCKS * LANES,
            bytes_accessed=2 * groups * height * DEPTH + 4 * height * BLOCKS * LANES,
            transcendentals=0,
        ),
        name="product",
    )(order, samples, *panels, *extra)


def per_device(records, record_tail, templates, channel_mask, lag_shift):
    me = lax.axis_index("tmpl")
    devices = lax.axis_size("tmpl")
    core = lax.axis_index("tm")
    cores = lax.axis_size("tm")
    channels = records.shape[0]
    groups = lag_shift.shape[0] // STEP
    half = groups // cores
    place = jnp.stack([me, core]).astype(jnp.int32)
    templates = templates.T
    channel_mask = channel_mask.T
    pairs = [(0, 1), (1, 0)]
    following = lax.ppermute(records, "tm", [(i + 1, i) for i in range(cores - 1)])
    closing, lag = stage(channels, record_tail.T, lag_shift, place)
    aligned = align(records, following, closing, lag, place)
    doubling = channels == STEP and devices == groups and devices & (devices - 1) == 0
    parts = []
    held = received = aligned[None]
    slots = [0]
    order = place if doubling else place * jnp.array([0, 1], jnp.int32)
    begun, received = lax.optimization_barrier((order, received))
    reach = groups // 2
    while reach:
        if doubling:
            if len(slots) > 1:
                held = jnp.concatenate([held, received], axis=0)
            received = lax.ppermute(held, "tmpl", [(i, i ^ reach) for i in range(devices)])
        if len(parts) < PARTS:
            part, weight = normalized(templates, channel_mask, begun, len(parts), half // PARTS)
            part, received, begun = lax.optimization_barrier((part, received, begun))
            parts.append(part)
        slots += [slot ^ reach for slot in slots]
        reach //= 2
    early, late = [(part, lax.ppermute(part, "tm", pairs)) for part in parts]
    if doubling:
        near, far = held, received
    else:
        held = lax.all_gather(aligned, "tmpl", axis=0)
        held = held[:, : SPANS * channels].reshape(groups, STEP // channels, SPANS, channels, LANES)
        held = jnp.moveaxis(held, 1, 2).reshape(groups, SPANS * STEP, LANES)
        held = jnp.pad(held, ((0, 0), (0, 4), (0, 0)))
        held = jnp.stack([held[slot] for slot in slots])
        near, far = held[:half], held[half:]
    total = product(order, near, early, slots[:half])
    return product(order, far, late, slots[half:], (weight, total))


def solution(mesh):
    placed = (P("tmpl", ("win", "tm")), P(None, "win"), P("tmpl", "tm"), P("tmpl", None), P("win"))
    return jax.shard_map(
        per_device, mesh=mesh, in_specs=placed, out_specs=P("tmpl", ("win", "tm")), check_vma=False
    )
```
